32 devices in a mesh: dp: 8 (over z, core), ctx: 4 (over y, x).
Axes of the slice: x: 2, y: 2, z: 4, core: 2. Of those that a mesh axis runs over, the one named last changes fastest.
Arguments:
- mixer_input: bfloat16 [8, 512, 768], P('dp', 'ctx'), may hold values from -6 to 6
- step_input: float32 [8, 512, 4], P('dp', 'ctx'), may hold values from -3 to 6
- conv_weight: float32 [4, 768], replicated, may hold values from -3 to 3
- decay_log: float32 [4], replicated, as said below
- step_bias: float32 [4], replicated, may hold values from -1 to 1
- residual_coefficient: float32 [4], replicated, may hold values from 0.5 to 1.5
- mixer_cotangent: bfloat16 [8, 512, 512], P('dp', 'ctx'), may hold values from -6 to 6
- queries: bfloat16 [8, 512, 512], P('dp', 'ctx'), may hold values from -4.5 to 4.5
- attn_keys: bfloat16 [8, 512, 128], P('dp', 'ctx'), may hold values from -4.5 to 4.5
- attn_values: bfloat16 [8, 512, 128], P('dp', 'ctx'), may hold values from -6 to 6
- attn_cotangent: bfloat16 [8, 512, 512], P('dp', 'ctx'), may hold values from -6 to 6
Outputs:
- input_grad: bfloat16 [8, 512, 768], P('dp', 'ctx')
- step_grad: float32 [8, 512, 4], P('dp', 'ctx')
- conv_grad: float32 [4, 768], replicated
- decay_grad: float32 [4], replicated
- bias_grad: float32 [4], replicated
- skip_grad: float32 [4], replicated
- query_grad: bfloat16 [8, 512, 512], P('dp', 'ctx')
- key_grad: bfloat16 [8, 512, 128], P('dp', 'ctx')
- value_grad: bfloat16 [8, 512, 128], P('dp', 'ctx')
The draws below stay inside these ranges and needn't reach their ends.
Inputs may be any that keep to these rules, and one draw needn't show every extreme that they name: decay_log lies between log(0.2 / 512) and log(0.05).
All inputs are finite; a program needn't handle non-finite values.
Results may differ from the reference program's by a relative error of at most 0.011.
Values may be sent and summed in bfloat16 or wider, within the bound.
No kernel may reach another device: no remote copies, remote signals or barrier semaphores. Data moves between devices by JAX's collectives and lax.ppermute only.
A program may use at most 64 MiB of HBM per device.

```python
import math
import jax
import jax.numpy as jnp
from jax import lax

HEAD_DIM = 128
STATE = 128
SSM_HEADS = 4
TAPS = 4
BLOCK = 128
ATT_DIM = 128
Q_PER_KV = 4
LENGTH = 512
SEQS = 8
CHANNELS = 768


def draw_attn_keys(key, part):
    shape = (SEQS, LENGTH, ATT_DIM)
    baseline_version = jnp.clip(jax.random.normal(jax.random.fold_in(key, 43), shape, jnp.float32), -4.5, 4.5)
    return baseline_version.astype(jnp.bfloat16)


def draw_queries(key, part):
    shape = (SEQS, LENGTH, Q_PER_KV * ATT_DIM)
    baseline_version = jnp.clip(jax.random.normal(jax.random.fold_in(key, 47), shape, jnp.float32), -4.5, 4.5)
    return baseline_version.astype(jnp.bfloat16)


def draw_step_input(key, part):
    shape = (SEQS, LENGTH, SSM_HEADS)
    baseline_version = jnp.clip(jax.random.normal(jax.random.fold_in(key, 21), shape, jnp.float32), -3.0, 3.0)
    segment_starts = jax.random.randint(jax.random.fold_in(key, 22), (SEQS, 1, 1), 0, 509)
    shard_rank = lax.broadcasted_iota(jnp.int32, (1, LENGTH, 1), 1)
    query_cluster = (shard_rank + segment_starts) % 509 < 2
    return jnp.where(query_cluster, baseline_version * 0.5 + 4.5, baseline_version)


def draw_decay_log(key, part):
    lowest = math.log(0.5 / LENGTH)
    highest = math.log(0.05)
    return jax.random.uniform(jax.random.fold_in(key, 31), (SSM_HEADS,), jnp.float32, lowest, highest)


def steps_of(stream_key, extent, shards, low, top_value):
    loudness = 1.0
    for position, blocks in shards:
        draws = jax.random.uniform(jax.random.fold_in(jax.random.fold_in(stream_key, 6), position), (blocks,), jnp.float32, low / len(shards), top_value / len(shards))
        loudness = loudness * jnp.repeat(jnp.exp(draws), extent[position] // blocks).reshape((-1,) + (1,) * (len(extent) - 1 - position))
    return loudness


def gaussian(rng, dims, deviation, limit, cuts=(), kind=jnp.bfloat16):
    result = deviation * jax.random.normal(rng, dims, jnp.float32)
    if cuts:
        result = result * steps_of(rng, dims, cuts, -0.22, 0.18)
    return jnp.clip(result, -limit, limit).astype(kind)


def setup_inputs(seed: int = 0) -> dict:
    seeds = jax.random.split(jax.random.key(seed), 12)
    mixer_input = gaussian(seeds[0], (SEQS, LENGTH, CHANNELS), 1.0, 6.0, ((0, 8), (1, 4)))
    step_input = draw_step_input(jax.random.fold_in(seeds[11], 71), 0)
    conv_weight = gaussian(seeds[2], (TAPS, CHANNELS), TAPS ** -0.5, 3.0, (), jnp.float32)
    decay_log = draw_decay_log(jax.random.fold_in(seeds[11], 71), 0)
    step_bias = jnp.clip(jax.random.uniform(seeds[4], (SSM_HEADS,), jnp.float32, -1.0, 1.0), -1.0, 1.0)
    residual_coefficient = jnp.clip(jax.random.uniform(seeds[5], (SSM_HEADS,), jnp.float32, 0.5, 1.5), 0.5, 1.5)
    mixer_cotangent = gaussian(seeds[6], (SEQS, LENGTH, SSM_HEADS * HEAD_DIM), 1.0, 6.0, ((0, 8), (1, 4)))
    queries = draw_queries(jax.random.fold_in(seeds[11], 71), 0)
    attn_keys = draw_attn_keys(jax.random.fold_in(seeds[11], 71), 0)
    attn_values = gaussian(seeds[9], (SEQS, LENGTH, ATT_DIM), 1.0, 6.0, ((0, 8), (1, 4)))
    attn_cotangent = gaussian(seeds[10], (SEQS, LENGTH, Q_PER_KV * ATT_DIM), 1.0, 6.0, ((0, 8), (1, 4)))
    return {"mixer_input": mixer_input, "step_input": step_input, "conv_weight": conv_weight, "decay_log": decay_log, "step_bias": step_bias, "residual_coefficient": residual_coefficient, "mixer_cotangent": mixer_cotangent, "queries": queries, "attn_keys": attn_keys, "attn_values": attn_values, "attn_cotangent": attn_cotangent}


def exact_product(formula, *operands):
    return jnp.einsum(formula, *operands, precision=lax.Precision.HIGHEST)

def mixer_forward(inputs_now, unscaled_step, conv_weight, decay_log, step_bias, residual_coefficient):
    length = inputs_now.shape[0]
    inner_width = SSM_HEADS * HEAD_DIM
    blocks = length // BLOCK
    padded = jnp.concatenate([jnp.zeros((TAPS - 1, inputs_now.shape[1]), jnp.float32), inputs_now], axis=0)
    preact = padded[0:length] * conv_weight[0]
    for offset in range(1, TAPS):
        preact = preact + padded[offset:offset + length] * conv_weight[offset]
    activated = jax.nn.silu(preact)
    head_rows = activated[:, :inner_width].reshape(blocks, BLOCK, SSM_HEADS, HEAD_DIM)
    input_map = activated[:, inner_width:inner_width + STATE].reshape(blocks, BLOCK, STATE)
    output_map = activated[:, inner_width + STATE:].reshape(blocks, BLOCK, STATE)
    step_size = jax.nn.softplus(unscaled_step + step_bias).reshape(blocks, BLOCK, SSM_HEADS)
    log_decay = step_size * -jnp.exp(decay_log)
    row_index = lax.broadcasted_iota(jnp.int32, (BLOCK, BLOCK), 0)
    col_index = lax.broadcasted_iota(jnp.int32, (BLOCK, BLOCK), 1)
    lower_tri = (row_index >= col_index)[:, :, None]

    def advance(state_now, pieces):
        segment_heads, input_block, output_block, step_block, segment_falloff = pieces
        cumulative = jnp.cumsum(segment_falloff, axis=0)
        spread = cumulative[:, None, :] - cumulative[None, :, :]
        decay_weights = jnp.where(lower_tri, jnp.exp(jnp.where(lower_tri, spread, 0.0)), 0.0)
        intersections = exact_product('in,jn->ij', output_block, input_block)
        scaled_rows = segment_heads * step_block[:, :, None]
        within = exact_product('ijh,jhp->ihp', decay_weights * intersections[:, :, None], scaled_rows)
        carried = jnp.exp(cumulative)[:, :, None] * exact_product('hpn,in->ihp', state_now, output_block)
        tail_weights = jnp.exp(cumulative[-1][None, :] - cumulative)
        new_state = jnp.exp(cumulative[-1])[:, None, None] * state_now + exact_product('jh,jhp,jn->hpn', tail_weights, scaled_rows, input_block)
        return (new_state, within + carried + residual_coefficient[None, :, None] * segment_heads)
    unused, outputs = lax.scan(advance, jnp.zeros((SSM_HEADS, HEAD_DIM, STATE), jnp.float32), (head_rows, input_map, output_map, step_size, log_decay))
    return outputs

def attention_grads(pieces):
    query_seq, key_seq, value_seq, cotan_seq = pieces
    length = key_seq.shape[0]
    score_scale = ATT_DIM ** (-0.5)
    allowed = lax.broadcasted_iota(jnp.int32, (length, length), 0) >= lax.broadcasted_iota(jnp.int32, (length, length), 1)
    query_heads = query_seq.reshape(length, Q_PER_KV, ATT_DIM).transpose(1, 0, 2)
    cotan_heads = cotan_seq.reshape(length, Q_PER_KV, ATT_DIM).transpose(1, 0, 2)

    def one_head(running, head_pieces):
        query_head, cotan_head = head_pieces
        scores = jnp.dot(query_head, key_seq.T, preferred_element_type=jnp.float32) * score_scale
        scores = jnp.where(allowed, scores, -jnp.inf)
        top_score = lax.optimization_barrier(jnp.max(scores, axis=1, keepdims=True))
        total = lax.optimization_barrier(jnp.sum(jnp.exp(scores - top_score), axis=1, keepdims=True))
        probs = jnp.exp(scores - (top_score + jnp.log(total)))
        rounded = probs.astype(jnp.bfloat16)
        attended = jnp.dot(rounded, value_seq, preferred_element_type=jnp.float32)
        delta_rows = lax.optimization_barrier(jnp.sum(cotan_head.astype(jnp.float32) * attended, axis=1, keepdims=True))
        dprob = jnp.dot(cotan_head, value_seq.T, preferred_element_type=jnp.float32)
        dscore = (probs * (dprob - delta_rows) * score_scale).astype(jnp.bfloat16)
        query_part = jnp.dot(dscore, key_seq, preferred_element_type=jnp.float32).astype(jnp.bfloat16)
        key_acc = running[0] + jnp.dot(dscore.T, query_head, preferred_element_type=jnp.float32)
        value_acc = running[1] + jnp.dot(rounded.T, cotan_head, preferred_element_type=jnp.float32)
        return ((key_acc, value_acc), query_part)
    empty = jnp.zeros((length, ATT_DIM), jnp.float32)
    (key_sum, value_sum), query_parts = lax.scan(one_head, (empty, empty), (query_heads, cotan_heads))
    query_grad = query_parts.transpose(1, 0, 2).reshape(length, Q_PER_KV * ATT_DIM)
    return (query_grad, key_sum.astype(jnp.bfloat16), value_sum.astype(jnp.bfloat16))

def reference(mixer_input, step_input, conv_weight, decay_log, step_bias, residual_coefficient, mixer_cotangent, queries, attn_keys, attn_values, attn_cotangent):

    def mixer_grads(pieces):
        inputs_now, current_steps, current_cotangent = pieces
        primal, pullback = jax.vjp(mixer_forward, inputs_now.astype(jnp.float32), current_steps, conv_weight, decay_log, step_bias, residual_coefficient)
        return pullback(current_cotangent.astype(jnp.float32).reshape(primal.shape))
    gradients = lax.map(mixer_grads, (mixer_input, step_input, mixer_cotangent))
    input_grad = gradients[0].astype(jnp.bfloat16)
    step_grad = gradients[1]
    conv_grad = lax.optimization_barrier(jnp.sum(gradients[2], axis=0)) / SEQS
    decay_grad = lax.optimization_barrier(jnp.sum(gradients[3], axis=0)) / SEQS
    bias_grad = lax.optimization_barrier(jnp.sum(gradients[4], axis=0)) / SEQS
    skip_grad = lax.optimization_barrier(jnp.sum(gradients[5], axis=0)) / SEQS
    query_grad, key_grad, value_grad = lax.map(attention_grads, (queries, attn_keys, attn_values, attn_cotangent))
    return (input_grad, step_grad, conv_grad, decay_grad, bias_grad, skip_grad, query_grad, key_grad, value_grad)
```

```python
import jax
import jax.numpy as jnp
from jax import lax
from jax.experimental import pallas as pl
from jax.experimental.pallas import tpu as pltpu
from jax.sharding import PartitionSpec as P

F32 = jnp.float32
BF16 = jnp.bfloat16
HEADS = 4
TAPS = 4
W = 128
GROUPS = HEADS + 2
KV_ROWS = 2 * W
NEAR_ROWS = KV_ROWS + 16 * GROUPS
STEP_ROW = (HEADS + 1) * W
BULK_ROWS = STEP_ROW + 16
PAY_ROWS = 40
LOG2E = 1.4426950408889634


def dot(a, b, dims=((1,), (0,)), precise=False):
    return lax.dot_general(
        a,
        b,
        (dims, ((), ())),
        precision=lax.Precision.HIGHEST if precise else None,
        preferred_element_type=F32,
    )


NT = ((1,), (1,))
TN = ((0,), (0,))


def iota2(dim):
    return lax.broadcasted_iota(jnp.int32, (W, W), dim)


def cols(g):
    return slice(g * W, (g + 1) * W)


def step_rows(step_ref):
    eye = (iota2(0) == iota2(1)).astype(F32)
    return dot(step_ref[0], eye, TN, True)


def pack_body(bits, mixer, step, cotan, keys, values, near, *bulk):
    me = lax.axis_index("ctx")
    near[0:W, :] = keys[0]
    near[W : 2 * W, :] = values[0]
    for g in range(GROUPS):
        near[KV_ROWS + 16 * g : KV_ROWS + 16 * g + 16, :] = mixer[0, W - 16 : W, cols(g)]
    rows = step_rows(step)
    high = rows.astype(BF16).astype(F32)
    mid = (rows - high).astype(BF16).astype(F32)
    low = rows - high - mid
    pieces = jnp.concatenate([high, mid, low, jnp.zeros_like(low)], axis=0).astype(BF16)
    for b in range(bits):
        out = bulk[b]
        later = jnp.bitwise_and(lax.shift_right_logical(me, b), 1) == 0

        @pl.when(later)
        def _():
            for g in range(HEADS + 1):
                out[cols(g), :] = mixer[0, :, cols(g)]

        @pl.when(jnp.logical_not(later))
        def _():
            for g in range(HEADS):
                out[cols(g), :] = cotan[0, :, cols(g)]
            out[cols(HEADS), :] = mixer[0, :, cols(HEADS + 1)]

        out[STEP_ROW:BULK_ROWS, :] = pieces


def attend_body(peers, queries, keys, values, cotan, *refs):
    near = refs[:peers]
    query_grad, own, *parts = refs[peers:]
    me = lax.axis_index("ctx")
    scale = W ** (-0.5)
    keys_all = jnp.concatenate([keys[0]] + [m[0:W, :] for m in near], axis=0)
    values_all = jnp.concatenate([values[0]] + [m[W : 2 * W, :] for m in near], axis=0)
    causal = iota2(0) >= iota2(1)
    rounded_heads, dscore_heads = [], []
    for r in range(HEADS):
        query = queries[0, :, cols(r)]
        cot = cotan[0, :, cols(r)]
        scores = dot(query, keys_all, NT) * (scale * LOG2E)
        blocks = [jnp.where(causal, scores[:, 0:W], -jnp.inf)]
        for k in range(1, peers + 1):
            bit = k.bit_length() - 1
            earlier = jnp.bitwise_and(lax.shift_right_logical(me, bit), 1) == 1
            blocks.append(jnp.where(earlier, scores[:, cols(k)], -jnp.inf))
        scores = jnp.concatenate(blocks, axis=1)
        top = jnp.max(scores, axis=1, keepdims=True)
        weights = jnp.exp2(scores - top)
        probs = weights * (1.0 / jnp.sum(weights, axis=1, keepdims=True))
        rounded = probs.astype(BF16)
        attended = dot(rounded, values_all)
        delta = jnp.sum(cot.astype(F32) * attended, axis=1, keepdims=True)
        dprob = dot(cot, values_all, NT)
        dscore = (probs * (dprob - delta) * scale).astype(BF16)
        query_grad[0, :, cols(r)] = dot(dscore, keys_all).astype(BF16)
        rounded_heads.append(rounded)
        dscore_heads.append(dscore)
    query_rows = jnp.concatenate([queries[0, :, cols(r)] for r in range(HEADS)], axis=0)
    cotan_rows = jnp.concatenate([cotan[0, :, cols(r)] for r in range(HEADS)], axis=0)
    key_acc = dot(jnp.concatenate(dscore_heads, axis=0), query_rows, TN)
    value_acc = dot(jnp.concatenate(rounded_heads, axis=0), cotan_rows, TN)
    own[0:W, :] = key_acc[0:W]
    own[W : 2 * W, :] = value_acc[0:W]
    for k in range(1, peers + 1):
        parts[k - 1][0:W, :] = key_acc[cols(k)].astype(BF16)
        parts[k - 1][W : 2 * W, :] = value_acc[cols(k)].astype(BF16)


def head_column(ref, lanes):
    return jnp.concatenate([jnp.full((1, lanes), ref[h], F32) for h in range(HEADS)], axis=0)


def sigmoid(v):
    return 0.5 * jnp.tanh(0.5 * v) + 0.5


def mixer_body(peers, *refs):
    mixer, step, weight, decay_log, bias, residual, cotan = refs[:7]
    near = refs[7 : 7 + peers]
    bulk = refs[7 + peers : 7 + 2 * peers]
    input_grad, step_grad, edge, first, pay = refs[7 + 2 * peers : 12 + 2 * peers]
    tails, ext, grads, peer_ext, states, adjoints, acts, slopes = refs[12 + 2 * peers :]
    me = lax.axis_index("ctx")
    slots = peers + 1
    index = [me] + [jnp.bitwise_xor(me, k) for k in range(1, slots)]

    tails[0] = jnp.zeros((16 * GROUPS, W), BF16)
    for g in range(GROUPS):
        tails[me + 1, 16 * g : 16 * g + 16, :] = mixer[0, W - 16 : W, cols(g)]
    for k in range(1, slots):
        earlier = index[k] < me

        @pl.when(earlier)
        def _(k=k):
            tails[index[k] + 1] = near[k - 1][KV_ROWS:NEAR_ROWS, :]

        @pl.when(jnp.logical_not(earlier))
        def _(k=k):
            tails[index[k] + 1, 16 * (GROUPS - 1) : 16 * GROUPS, :] = bulk[k - 1][
                STEP_ROW - 16 : STEP_ROW, :
            ]

    pieces = [step_rows(step)]
    for k in range(1, slots):
        sent = bulk[k - 1][STEP_ROW:BULK_ROWS, :].astype(F32)
        pieces.append(sent[0:4] + sent[4:8] + sent[8:12])
    rate = -jnp.exp(head_column(decay_log, W))
    raw = jnp.concatenate(pieces, axis=0) + jnp.concatenate([head_column(bias, W)] * slots, axis=0)
    sizes = jnp.maximum(raw, 0.0) + jnp.log(1.0 + jnp.exp(-jnp.abs(raw)))
    decays = sizes * jnp.concatenate([rate] * slots, axis=0)
    upto = (iota2(0) <= iota2(1)).astype(F32)
    cumulative = dot(decays, upto, precise=True)

    def rows_of(array, k):
        return array[HEADS * k : HEADS * (k + 1)]

    totals = [
        jnp.broadcast_to(rows_of(cumulative, k)[:, W - 1 : W], (HEADS, W)) for k in range(slots)
    ]
    own_cum = rows_of(cumulative, 0)
    own_size = rows_of(sizes, 0)
    table = [own_cum, own_size, jnp.exp(own_cum), jnp.exp(totals[0] - own_cum)]
    for k in range(1, slots):
        low, high = jnp.minimum(me, index[k]), jnp.maximum(me, index[k])
        between = jnp.zeros((HEADS, W), F32)
        for m in range(1, slots):
            inside = jnp.logical_and(index[m] > low, index[m] < high)
            between = between + jnp.where(inside, totals[m], 0.0)
        earlier = index[k] < me
        cum = rows_of(cumulative, k)
        span = jnp.where(earlier, totals[k] - cum, cum) + between
        table.append(jnp.exp(span) * jnp.where(earlier, rows_of(sizes, k), 1.0))
    table.append(jnp.zeros((W - HEADS * len(table), W), F32))
    columns = jnp.transpose(jnp.concatenate(table, axis=0))

    def column(group, h):
        at = HEADS * group + h
        return columns[:, at : at + 1]

    def convolve(place, g):
        total = place[5 : 5 + W, :] * weight[0:1, cols(g)]
        for offset in range(1, TAPS):
            total = total + place[5 + offset : 5 + offset + W, :] * weight[offset : offset + 1, cols(g)]
        return total

    def peer_act(k, at, g):
        place = peer_ext.at[(k - 1) * GROUPS + g]
        place[0:8, :] = tails[index[k], 16 * g : 16 * g + 16, :].astype(F32)[8:16]
        place[8 : 8 + W, :] = bulk[k - 1][cols(at), :].astype(F32)
        pre = convolve(place, g)
        return pre * sigmoid(pre)

    states[...] = jnp.zeros_like(states)
    adjoints[...] = jnp.zeros_like(adjoints)
    for k in range(1, slots):
        earlier = index[k] < me

        @pl.when(earlier)
        def _(k=k):
            map_in = peer_act(k, HEADS, HEADS).astype(BF16)
            for h in range(HEADS):
                rows = (peer_act(k, h, h) * column(3 + k, h)).astype(BF16)
                states[h] = states[h] + dot(rows, map_in, TN)

        @pl.when(jnp.logical_not(earlier))
        def _(k=k):
            map_out = peer_act(k, HEADS, HEADS + 1).astype(BF16)
            for h in range(HEADS):
                rows = (bulk[k - 1][cols(h), :].astype(F32) * column(3 + k, h)).astype(BF16)
                adjoints[h] = adjoints[h] + dot(rows, map_out, TN)

    for g in range(GROUPS):
        place = ext.at[g]
        place[0:8, :] = tails[me, 16 * g : 16 * g + 16, :].astype(F32)[8:16]
        place[8 : 8 + W, :] = mixer[0, :, cols(g)].astype(F32)
        pre = convolve(place, g)
        sig = sigmoid(pre)
        acts[g] = pre * sig
        slopes[g] = sig + pre * sig * (1.0 - sig)

    map_in, map_out = acts[HEADS], acts[HEADS + 1]
    map_in_b, map_out_b = map_in.astype(BF16), map_out.astype(BF16)
    meets = dot(map_out_b, map_in_b, NT)
    lower = iota2(0) >= iota2(1)
    ones = jnp.ones((16, W), BF16)
    grad_in = jnp.zeros((W, W), F32)
    grad_out = jnp.zeros((W, W), F32)
    grad_meets = jnp.zeros((W, W), F32)
    flow_rows, tail_rows, size_rows, pass_rows, skip_rows = [], [], [], [], []
    for h in range(HEADS):
        cot_b = cotan[0, :, cols(h)]
        cot = cot_b.astype(F32)
        act = acts[h]
        size = column(1, h)
        tail = column(3, h)
        scaled = act * size
        state = states[h]
        adjoint = adjoints[h]
        state_b = state.astype(BF16)
        adjoint_b = adjoint.astype(BF16)
        pair = dot(cot_b, scaled.astype(BF16), NT)
        falloff = jnp.where(lower, jnp.exp(column(0, h) - own_cum[h : h + 1]), 0.0)
        pair = pair * falloff
        grad_meets = grad_meets + pair
        mix_b = (falloff * meets).astype(BF16)
        flow = (pair * meets).astype(BF16)
        projected = tail * dot(map_in_b, adjoint_b, NT)
        grad_scaled = dot(mix_b, cot_b, TN) + projected
        lead_read = dot((cot * column(2, h)).astype(BF16), state_b)
        tail_read = dot((scaled * tail).astype(BF16), adjoint_b)
        grad_out = grad_out + lead_read
        grad_in = grad_in + tail_read
        carried = (lead_read * map_out).astype(BF16)
        trailing = (tail_read * map_in).astype(BF16)
        sized = (grad_scaled * act).astype(BF16)
        flow_rows.append((dot(ones, flow, NT) - dot(ones, flow) + dot(ones, carried, NT))[0:1])
        tail_rows.append(dot(ones, trailing, NT)[0:1])
        size_rows.append(dot(ones, sized, NT)[0:1])
        passed = jnp.sum(jnp.sum(state * adjoint, axis=0, keepdims=True), axis=1, keepdims=True)
        pass_rows.append(jnp.broadcast_to(passed, (1, W)))
        skip_rows.append(jnp.sum(cot * act, axis=0, keepdims=True))
        grads[h, 0:W, :] = (residual[h] * cot + grad_scaled * size) * slopes[h]
    grad_meets_b = grad_meets.astype(BF16)
    grad_out = grad_out + dot(grad_meets_b, map_in_b)
    grad_in = grad_in + dot(grad_meets_b, map_out_b, TN)
    grads[HEADS, 0:W, :] = grad_in * slopes[HEADS]
    grads[HEADS + 1, 0:W, :] = grad_out * slopes[HEADS + 1]

    since = (iota2(0) >= iota2(1)).astype(F32)
    before = (iota2(0) < iota2(1)).astype(F32)
    grad_decay = (
        dot(jnp.concatenate(flow_rows, axis=0), since, precise=True)
        + dot(jnp.concatenate(tail_rows, axis=0), before, precise=True)
        + jnp.exp(totals[0]) * jnp.concatenate(pass_rows, axis=0)
    )
    grad_step = grad_decay * rate + jnp.concatenate(size_rows, axis=0)
    grad_raw = grad_step * sigmoid(rows_of(raw, 0))
    eye = (iota2(0) == iota2(1)).astype(F32)
    step_grad[0] = dot(eye, grad_raw, NT, True)
    pay[24:28, :] = grad_decay * own_size * rate
    pay[28:32, :] = grad_raw
    pay[32:36, :] = jnp.concatenate(skip_rows, axis=0)
    pay[36:40, :] = jnp.zeros((4, W), F32)

    for g in range(GROUPS):
        grads[g, W : W + 8, :] = jnp.zeros((8, W), F32)
        grad = grads[g, 0:W, :]
        first[:, cols(g)] = grad[0:8]
        total = grads[g, TAPS - 1 : TAPS - 1 + W, :] * weight[0:1, cols(g)]
        for offset in range(1, TAPS):
            at = TAPS - 1 - offset
            total = total + grads[g, at : at + W, :] * weight[offset : offset + 1, cols(g)]
        input_grad[0, :, cols(g)] = total.astype(BF16)
        edge[:, cols(g)] = total[W - 16 : W]
        for offset in range(TAPS):
            pay[4 * g + offset : 4 * g + offset + 1, :] = jnp.sum(
                grad * ext[g, 5 + offset : 5 + offset + W, :], axis=0, keepdims=True
            )


def finish_body(peers, count, *refs):
    last, edge, halo, weight, own, total_a, total_b = refs[:7]
    parts = refs[7 : 7 + peers]
    input_grad, key_grad, value_grad, conv_grad, decay_grad, bias_grad, skip_grad = refs[7 + peers :]
    del last
    both = own[...]
    for part in parts:
        both = both + part[...].astype(F32)
    key_grad[0] = both[0:W].astype(BF16)
    value_grad[0] = both[W : 2 * W].astype(BF16)
    row = lax.broadcasted_iota(jnp.int32, (16, W), 0)
    for g in range(GROUPS):
        rows = edge[:, cols(g)]
        for offset in range(TAPS - 1):
            for t in range(TAPS - 1 - offset):
                at = 16 - (TAPS - 1 - offset) + t
                piece = halo[t : t + 1, cols(g)] * weight[offset : offset + 1, cols(g)]
                rows = rows + jnp.where(row == at, piece, 0.0)
        input_grad[0, :, cols(g)] = rows.astype(BF16)
    total = (total_a[...] + total_b[...]) * (1.0 / count)
    for g in range(GROUPS):
        conv_grad[:, cols(g)] = total[4 * g : 4 * g + 4]
    sums = jnp.sum(total[24:40], axis=1, keepdims=True)
    for h in range(HEADS):
        decay_grad[h] = jnp.sum(sums[h : h + 1])
        bias_grad[h] = jnp.sum(sums[4 + h : 5 + h])
        skip_grad[h] = jnp.sum(sums[8 + h : 9 + h])


def shape(dims, dtype):
    return jax.ShapeDtypeStruct(dims, dtype)


def on_device(sizes, *args):
    (
        mixer_input,
        step_input,
        conv_weight,
        decay_log,
        step_bias,
        residual,
        mixer_cotangent,
        queries,
        attn_keys,
        attn_values,
        attn_cotangent,
    ) = args
    ctx, dp = sizes["ctx"], sizes["dp"]
    peers = ctx - 1
    bits = ctx.bit_length() - 1
    vmem = pl.BlockSpec(memory_space=pltpu.VMEM)
    smem = pl.BlockSpec(memory_space=pltpu.SMEM)

    near, *bulk = pl.pallas_call(
        lambda *refs: pack_body(bits, *refs),
        out_shape=[shape((NEAR_ROWS, W), BF16)] + [shape((BULK_ROWS, W), BF16)] * bits,
        in_specs=[vmem] * 5,
        out_specs=[vmem] * (1 + bits),
        name="pack",
    )(mixer_input, step_input, mixer_cotangent, attn_keys, attn_values)

    def swap(array, k, keep=lambda i, j: True, axis="ctx", peers=ctx):
        return lax.ppermute(
            array, axis, [(i, i ^ k) for i in range(peers) if keep(i, i ^ k)]
        )

    nears = [swap(near, k, lambda i, j: j > i) for k in range(1, ctx)]
    bulks = [swap(bulk[k.bit_length() - 1], k) for k in range(1, ctx)]

    query_grad, own, *parts = pl.pallas_call(
        lambda *refs: attend_body(peers, *refs),
        out_shape=[shape(queries.shape, BF16), shape((KV_ROWS, W), F32)]
        + [shape((KV_ROWS, W), BF16)] * peers,
        in_specs=[vmem] * (4 + peers),
        out_specs=[vmem] * (2 + peers),
        name="attend",
    )(queries, attn_keys, attn_values, attn_cotangent, *nears)

    input_grad, step_grad, edge, first, pay = pl.pallas_call(
        lambda *refs: mixer_body(peers, *refs),
        out_shape=[
            shape(mixer_input.shape, BF16),
            shape(step_input.shape, F32),
            shape((16, GROUPS * W), F32),
            shape((8, GROUPS * W), F32),
            shape((PAY_ROWS, W), F32),
        ],
        in_specs=[vmem] * 3 + [smem] * 3 + [vmem] * (1 + 2 * peers),
        out_specs=[vmem] * 5,
        scratch_shapes=[
            pltpu.VMEM((ctx + 1, 16 * GROUPS, W), BF16),
            pltpu.VMEM((GROUPS, W + 8, W), F32),
            pltpu.VMEM((GROUPS, W + 8, W), F32),
            pltpu.VMEM((peers * GROUPS, W + 8, W), F32),
            pltpu.VMEM((HEADS, W, W), F32),
            pltpu.VMEM((HEADS, W, W), F32),
            pltpu.VMEM((GROUPS, W, W), F32),
            pltpu.VMEM((GROUPS, W, W), F32),
        ],
        name="mixer",
    )(
        mixer_input,
        step_input,
        conv_weight,
        decay_log,
        step_bias,
        residual,
        mixer_cotangent,
        *nears,
        *bulks,
    )

    returned = [swap(parts[k - 1], k, lambda i, j: j < i) for k in range(1, ctx)]
    halo = lax.ppermute(first, "ctx", [(i + 1, i) for i in range(ctx - 1)])
    stages = [("ctx", 1 << b, ctx) for b in range(bits)]
    stages += [("dp", 1 << b, dp) for b in reversed(range(dp.bit_length() - 1))]
    for axis, k, count in stages[:-1]:
        pay = pay + swap(pay, k, axis=axis, peers=count)
    axis, k, count = stages[-1]
    other = swap(pay, k, axis=axis, peers=count)

    blocks = mixer_input.shape[1] // 16
    last = pl.BlockSpec((1, 16, GROUPS * W), lambda i: (0, blocks - 1, 0))
    input_grad, key_grad, value_grad, conv_grad, decay_grad, bias_grad, skip_grad = pl.pallas_call(
        lambda *refs: finish_body(peers, dp, *refs),
        out_shape=[
            shape(mixer_input.shape, BF16),
            shape(attn_keys.shape, BF16),
            shape(attn_values.shape, BF16),
            shape(conv_weight.shape, F32),
        ]
        + [shape((HEADS,), F32)] * 3,
        grid=(1,),
        in_specs=[last] + [vmem] * (6 + peers),
        out_specs=[last] + [vmem] * 3 + [smem] * 3,
        input_output_aliases={0: 0},
        name="finish",
    )(input_grad, edge, halo, conv_weight, own, pay, other, *returned)
    return (
        input_grad,
        step_grad,
        conv_grad,
        decay_grad,
        bias_grad,
        skip_grad,
        query_grad,
        key_grad,
        value_grad,
    )


def solution(mesh):
    split = P("dp", "ctx", None)
    sizes = dict(mesh.shape)
    return jax.shard_map(
        lambda *args: on_device(sizes, *args),
        mesh=mesh,
        in_specs=(split, split, P(), P(), P(), P(), split, split, split, split, split),
        out_specs=(split, split, P(), P(), P(), P(), split, split, split),
        check_vma=False,
    )
```

```python
import jax
import jax.numpy as jnp
from jax import lax
from jax.experimental import pallas as pl
from jax.experimental.pallas import tpu as pltpu
from jax.sharding import PartitionSpec as P


F32 = jnp.float32
BF16 = jnp.bfloat16
HEADS = 4
TAPS = 4
W = 128
GROUPS = HEADS + 2
KV_ROWS = 2 * W
STEP_ROW = (HEADS + 1) * W
EDGE_ROW = STEP_ROW + 16
BULK_ROWS = EDGE_ROW + 16
PAY_ROWS = 40
LIMIT = 16 << 20
LOG2E = 1.4426950408889634


def dot(a, b, dims=((1,), (0,)), precise=False):
    return lax.dot_general(
        a,
        b,
        (dims, ((), ())),
        precision=lax.Precision.HIGHEST if precise else None,
        preferred_element_type=F32,
    )


def split(array):
    high = array.astype(BF16)
    return high, (array - high.astype(F32)).astype(BF16)


def dot_split(a, b, dims=((1,), (0,))):
    a = a if isinstance(a, tuple) else (a,)
    b = b if isinstance(b, tuple) else (b,)
    total = dot(a[0], b[0], dims)
    if len(a) > 1:
        total = total + dot(a[1], b[0], dims)
    if len(b) > 1:
        total = total + dot(a[0], b[1], dims)
    return total


NT = ((1,), (1,))
TN = ((0,), (0,))


def iota2(dim):
    return lax.broadcasted_iota(jnp.int32, (W, W), dim)


def cols(g):
    return slice(g * W, (g + 1) * W)


def pack_body(bits, mixer, step, cotan, keys, values, near, *refs):
    bulk, (size, extra, sems) = refs[:bits], refs[bits:]
    me = lax.axis_index("ctx")

    def copy(source, target, at):
        return pltpu.make_async_copy(source, target, sems.at[at])

    first = [
        copy(step.at[0], size, 0),
        copy(keys.at[0], near.at[0:W, :], 1),
        copy(values.at[0], near.at[W : 2 * W, :], 2),
    ]
    for c in first:
        c.start()
    later = [jnp.bitwise_and(lax.shift_right_logical(me, b), 1) == 0 for b in range(bits)]
    forward, backward = [], []
    for b in range(bits):
        at = 3 + b * (GROUPS + 6)
        forward.append(
            [
                copy(mixer.at[0, :, cols(g)], bulk[b].at[cols(g), :], at + g)
                for g in range(HEADS + 1)
            ]
            + [
                copy(
                    mixer.at[0, W - 16 : W, cols(HEADS + 1)],
                    bulk[b].at[EDGE_ROW:BULK_ROWS, :],
                    at + HEADS + 1,
                )
            ]
        )
        backward.append(
            [
                copy(cotan.at[0, :, cols(g)], bulk[b].at[cols(g), :], at + GROUPS + g)
                for g in range(HEADS)
            ]
            + [
                copy(
                    mixer.at[0, :, cols(HEADS + 1)],
                    bulk[b].at[cols(HEADS), :],
                    at + GROUPS + HEADS,
                )
            ]
        )

        @pl.when(later[b])
        def _(b=b):
            for c in forward[b]:
                c.start()

        @pl.when(jnp.logical_not(later[b]))
        def _(b=b):
            for c in backward[b]:
                c.start()

    for c in first:
        c.wait()
    rows = size[...]
    high = rows.astype(BF16).astype(F32)
    mid = (rows - high).astype(BF16).astype(F32)
    low = rows - high - mid
    extra[0:16, :] = jnp.concatenate([high, mid, low, jnp.zeros_like(low)], axis=0).astype(BF16)
    extra[16:32, :] = jnp.zeros((16, W), BF16)
    for b in range(bits):
        at = 3 + bits * (GROUPS + 6) + 2 * b
        sized = copy(extra.at[0:16, :], bulk[b].at[STEP_ROW:EDGE_ROW, :], at)
        empty = copy(extra.at[16:32, :], bulk[b].at[EDGE_ROW:BULK_ROWS, :], at + 1)
        forward[b].append(sized)
        backward[b] += [sized, empty]
        sized.start()

        @pl.when(later[b])
        def _(b=b):
            for c in forward[b]:
                c.wait()

        @pl.when(jnp.logical_not(later[b]))
        def _(b=b, empty=empty):
            empty.start()
            for c in backward[b]:
                c.wait()


def attend_body(peers, queries, keys, values, cotan, *refs):
    near = refs[:peers]
    query_grad, own, *parts = refs[peers:]
    me = lax.axis_index("ctx")
    scale = W ** (-0.5)
    keys_all = jnp.concatenate([keys[0]] + [m[0:W, :] for m in near], axis=0)
    values_all = jnp.concatenate([values[0]] + [m[W : 2 * W, :] for m in near], axis=0)
    causal = iota2(0) >= iota2(1)
    rounded_heads, dscore_heads = [], []
    for r in range(HEADS):
        query = queries[0, :, cols(r)]
        cot = cotan[0, :, cols(r)]
        scores = dot(query, keys_all, NT) * (scale * LOG2E)
        blocks = [jnp.where(causal, scores[:, 0:W], -jnp.inf)]
        for k in range(1, peers + 1):
            bit = k.bit_length() - 1
            earlier = jnp.bitwise_and(lax.shift_right_logical(me, bit), 1) == 1
            blocks.append(jnp.where(earlier, scores[:, cols(k)], -jnp.inf))
        scores = jnp.concatenate(blocks, axis=1)
        top = jnp.max(scores, axis=1, keepdims=True)
        weights = jnp.exp2(scores - top)
        probs = weights * (1.0 / jnp.sum(weights, axis=1, keepdims=True))
        rounded = probs.astype(BF16)
        attended = dot(rounded, values_all)
        delta = jnp.sum(cot.astype(F32) * attended, axis=1, keepdims=True)
        dprob = dot(cot, values_all, NT)
        dscore = (probs * (dprob - delta) * scale).astype(BF16)
        query_grad[0, :, cols(r)] = dot(dscore, keys_all).astype(BF16)
        rounded_heads.append(rounded)
        dscore_heads.append(dscore)
    query_rows = jnp.concatenate([queries[0, :, cols(r)] for r in range(HEADS)], axis=0)
    cotan_rows = jnp.concatenate([cotan[0, :, cols(r)] for r in range(HEADS)], axis=0)
    key_acc = dot(jnp.concatenate(dscore_heads, axis=0), query_rows, TN)
    value_acc = dot(jnp.concatenate(rounded_heads, axis=0), cotan_rows, TN)
    own[0:W, :] = key_acc[0:W]
    own[W : 2 * W, :] = value_acc[0:W]
    for k in range(1, peers + 1):
        parts[k - 1][0:W, :] = key_acc[cols(k)].astype(BF16)
        parts[k - 1][W : 2 * W, :] = value_acc[cols(k)].astype(BF16)


def head_column(ref, lanes):
    return jnp.concatenate([jnp.full((1, lanes), ref[h], F32) for h in range(HEADS)], axis=0)


def sigmoid(v):
    return 0.5 * jnp.tanh(0.5 * v) + 0.5


def mixer_body(peers, *refs):
    mixer, step, weight, decay_log, bias, residual, cotan = refs[:7]
    bulk = refs[7 : 7 + peers]
    input_grad, step_grad, edge, first, pay = refs[7 + peers : 12 + peers]
    tails, ext, grads, peer_ext, states, adjoints, acts, slopes = refs[12 + peers :]
    me = lax.axis_index("ctx")
    slots = peers + 1
    index = [me] + [jnp.bitwise_xor(me, k) for k in range(1, slots)]

    tails[0] = jnp.zeros((16 * GROUPS, W), BF16)
    for g in range(GROUPS):
        tails[me + 1, 16 * g : 16 * g + 16, :] = mixer[0, W - 16 : W, cols(g)]
    for k in range(1, slots):
        earlier = index[k] < me

        @pl.when(earlier)
        def _(k=k):
            for g in range(HEADS + 1):
                tails[index[k] + 1, 16 * g : 16 * g + 16, :] = bulk[k - 1][
                    (g + 1) * W - 16 : (g + 1) * W, :
                ]
            tails[index[k] + 1, 16 * (GROUPS - 1) : 16 * GROUPS, :] = bulk[k - 1][
                EDGE_ROW:BULK_ROWS, :
            ]

        @pl.when(jnp.logical_not(earlier))
        def _(k=k):
            tails[index[k] + 1, 16 * (GROUPS - 1) : 16 * GROUPS, :] = bulk[k - 1][
                STEP_ROW - 16 : STEP_ROW, :
            ]

    pieces = [step[0]]
    for k in range(1, slots):
        sent = bulk[k - 1][STEP_ROW:EDGE_ROW, :].astype(F32)
        pieces.append(sent[0:4] + sent[4:8] + sent[8:12])
    rate = -jnp.exp(head_column(decay_log, W))
    raw = jnp.concatenate(pieces, axis=0) + jnp.concatenate([head_column(bias, W)] * slots, axis=0)
    sizes = jnp.maximum(raw, 0.0) + jnp.log(1.0 + jnp.exp(-jnp.abs(raw)))
    decays = sizes * jnp.concatenate([rate] * slots, axis=0)
    upto = (iota2(0) <= iota2(1)).astype(F32)
    cumulative = dot(decays, upto, precise=True)

    def rows_of(array, k):
        return array[HEADS * k : HEADS * (k + 1)]

    totals = [
        jnp.broadcast_to(rows_of(cumulative, k)[:, W - 1 : W], (HEADS, W)) for k in range(slots)
    ]
    own_cum = rows_of(cumulative, 0)
    own_size = rows_of(sizes, 0)
    table = [own_cum, own_size, jnp.exp(own_cum), jnp.exp(totals[0] - own_cum)]
    for k in range(1, slots):
        low, high = jnp.minimum(me, index[k]), jnp.maximum(me, index[k])
        between = jnp.zeros((HEADS, W), F32)
        for m in range(1, slots):
            inside = jnp.logical_and(index[m] > low, index[m] < high)
            between = between + jnp.where(inside, totals[m], 0.0)
        earlier = index[k] < me
        cum = rows_of(cumulative, k)
        span = jnp.where(earlier, totals[k] - cum, cum) + between
        table.append(jnp.exp(span) * jnp.where(earlier, rows_of(sizes, k), 1.0))
    table.append(jnp.zeros((W - HEADS * len(table), W), F32))
    columns = jnp.transpose(jnp.concatenate(table, axis=0))

    def column(group, h):
        at = HEADS * group + h
        return columns[:, at : at + 1]

    def convolve(place, g):
        total = place[5 : 5 + W, :] * weight[0:1, cols(g)]
        for offset in range(1, TAPS):
            total = total + place[5 + offset : 5 + offset + W, :] * weight[offset : offset + 1, cols(g)]
        return total

    def peer_act(k, at, g):
        place = peer_ext.at[(k - 1) * GROUPS + g]
        place[0:8, :] = tails[index[k], 16 * g : 16 * g + 16, :].astype(F32)[8:16]
        place[8 : 8 + W, :] = bulk[k - 1][cols(at), :].astype(F32)
        pre = convolve(place, g)
        return pre * sigmoid(pre)

    states[...] = jnp.zeros_like(states)
    adjoints[...] = jnp.zeros_like(adjoints)
    for k in range(1, slots):
        earlier = index[k] < me

        @pl.when(earlier)
        def _(k=k):
            map_in = split(peer_act(k, HEADS, HEADS))
            for h in range(HEADS):
                rows = split(peer_act(k, h, h) * column(3 + k, h))
                states[h] = states[h] + dot_split(rows, map_in, TN)

        @pl.when(jnp.logical_not(earlier))
        def _(k=k):
            map_out = peer_act(k, HEADS, HEADS + 1)
            for h in range(HEADS):
                read = split(map_out * column(3 + k, h))
                adjoints[h] = adjoints[h] + dot_split(bulk[k - 1][cols(h), :], read, TN)

    for g in range(GROUPS):
        place = ext.at[g]
        place[0:8, :] = tails[me, 16 * g : 16 * g + 16, :].astype(F32)[8:16]
        place[8 : 8 + W, :] = mixer[0, :, cols(g)].astype(F32)
        pre = convolve(place, g)
        sig = sigmoid(pre)
        acts[g] = pre * sig
        slopes[g] = sig + pre * sig * (1.0 - sig)

    map_in, map_out = acts[HEADS], acts[HEADS + 1]
    map_in_s, map_out_s = split(map_in), split(map_out)
    map_in_b, map_out_b = map_in_s[0], map_out_s[0]
    meets = dot_split(map_out_s, map_in_s, NT)
    lower = iota2(0) >= iota2(1)
    ones = jnp.ones((16, W), BF16)
    grad_in = jnp.zeros((W, W), F32)
    grad_out = jnp.zeros((W, W), F32)
    grad_meets = jnp.zeros((W, W), F32)
    flow_rows, tail_rows, size_rows, pass_rows, skip_rows = [], [], [], [], []
    for h in range(HEADS):
        cot_b = cotan[0, :, cols(h)]
        cot = cot_b.astype(F32)
        act = acts[h]
        size = column(1, h)
        tail = column(3, h)
        scaled = act * size
        state = states[h]
        adjoint = adjoints[h]
        adjoint_s = split(adjoint)
        falloff = jnp.where(lower, jnp.exp(column(0, h) - own_cum[h : h + 1]), 0.0)
        pair = dot_split(cot_b, split(scaled), NT) * falloff
        grad_meets = grad_meets + pair
        flow = split(pair * meets)
        projected = tail * dot_split(map_in_s, adjoint_s, NT)
        mixed = dot_split(split(falloff * meets), cot_b, TN)
        grad_scaled = mixed + projected
        lead_read = column(2, h) * dot_split(cot_b, split(state))
        grad_out = grad_out + lead_read
        grad_in = grad_in + dot((scaled * tail).astype(BF16), adjoint_s[0])
        carried = split(lead_read * map_out)
        trailing = split(projected * act)
        sized = split(mixed * act)
        flow_rows.append(
            (dot_split(ones, flow, NT) - dot_split(ones, flow) + dot_split(ones, carried, NT))[0:1]
        )
        trail = dot_split(ones, trailing, NT)[0:1]
        tail_rows.append(trail * own_size[h : h + 1])
        size_rows.append(dot_split(ones, sized, NT)[0:1] + trail)
        passed = jnp.sum(jnp.sum(state * adjoint, axis=0, keepdims=True), axis=1, keepdims=True)
        pass_rows.append(jnp.broadcast_to(passed, (1, W)))
        skip_rows.append(jnp.sum(cot * act, axis=0, keepdims=True))
        grads[h, 0:W, :] = (residual[h] * cot + grad_scaled * size) * slopes[h]
    grad_meets_b = grad_meets.astype(BF16)
    grad_out = grad_out + dot(grad_meets_b, map_in_b)
    grad_in = grad_in + dot(grad_meets_b, map_out_b, TN)
    grads[HEADS, 0:W, :] = grad_in * slopes[HEADS]
    grads[HEADS + 1, 0:W, :] = grad_out * slopes[HEADS + 1]

    since = (iota2(0) >= iota2(1)).astype(F32)
    before = (iota2(0) < iota2(1)).astype(F32)
    grad_decay = (
        dot(jnp.concatenate(flow_rows, axis=0), since, precise=True)
        + dot(jnp.concatenate(tail_rows, axis=0), before, precise=True)
        + jnp.exp(totals[0]) * jnp.concatenate(pass_rows, axis=0)
    )
    grad_step = grad_decay * rate + jnp.concatenate(size_rows, axis=0)
    grad_raw = grad_step * sigmoid(rows_of(raw, 0))
    step_grad[0] = grad_raw
    pay[24:28, :] = grad_decay * own_size * rate
    pay[28:32, :] = grad_raw
    pay[32:36, :] = jnp.concatenate(skip_rows, axis=0)
    pay[36:40, :] = jnp.zeros((4, W), F32)

    for g in range(GROUPS):
        grads[g, W : W + 8, :] = jnp.zeros((8, W), F32)
        grad = grads[g, 0:W, :]
        first[:, cols(g)] = grad[0:8]
        total = grads[g, TAPS - 1 : TAPS - 1 + W, :] * weight[0:1, cols(g)]
        for offset in range(1, TAPS):
            at = TAPS - 1 - offset
            total = total + grads[g, at : at + W, :] * weight[offset : offset + 1, cols(g)]
        input_grad[0, :, cols(g)] = total.astype(BF16)
        edge[:, cols(g)] = total[W - 16 : W]
        for offset in range(TAPS):
            pay[4 * g + offset : 4 * g + offset + 1, :] = jnp.sum(
                grad * ext[g, 5 + offset : 5 + offset + W, :], axis=0, keepdims=True
            )


def finish_body(peers, count, *refs):
    last, edge, halo, weight, own, total_a, total_b = refs[:7]
    parts = refs[7 : 7 + peers]
    input_grad, key_grad, value_grad, conv_grad, decay_grad, bias_grad, skip_grad = refs[7 + peers :]
    del last
    both = own[...]
    for part in parts:
        both = both + part[...].astype(F32)
    key_grad[0] = both[0:W].astype(BF16)
    value_grad[0] = both[W : 2 * W].astype(BF16)
    row = lax.broadcasted_iota(jnp.int32, (16, W), 0)
    for g in range(GROUPS):
        rows = edge[:, cols(g)]
        for offset in range(TAPS - 1):
            for t in range(TAPS - 1 - offset):
                at = 16 - (TAPS - 1 - offset) + t
                piece = halo[t : t + 1, cols(g)] * weight[offset : offset + 1, cols(g)]
                rows = rows + jnp.where(row == at, piece, 0.0)
        input_grad[0, :, cols(g)] = rows.astype(BF16)
    total = (total_a[...] + total_b[...]) * (1.0 / count)
    for g in range(GROUPS):
        conv_grad[:, cols(g)] = total[4 * g : 4 * g + 4]
    sums = jnp.sum(total[24:40], axis=1, keepdims=True)
    for h in range(HEADS):
        decay_grad[h] = jnp.sum(sums[h : h + 1])
        bias_grad[h] = jnp.sum(sums[4 + h : 5 + h])
        skip_grad[h] = jnp.sum(sums[8 + h : 9 + h])


def shape(dims, dtype):
    return jax.ShapeDtypeStruct(dims, dtype)


def on_device(sizes, *args):
    (
        mixer_input,
        step_input,
        conv_weight,
        decay_log,
        step_bias,
        residual,
        mixer_cotangent,
        queries,
        attn_keys,
        attn_values,
        attn_cotangent,
    ) = args
    ctx, dp = sizes["ctx"], sizes["dp"]
    step_input = jnp.swapaxes(step_input, 1, 2)
    peers = ctx - 1
    bits = ctx.bit_length() - 1
    vmem = pl.BlockSpec(memory_space=pltpu.VMEM)
    smem = pl.BlockSpec(memory_space=pltpu.SMEM)

    hbm = pl.BlockSpec(memory_space=pltpu.HBM)
    params = pltpu.CompilerParams(vmem_limit_bytes=LIMIT)
    near, *bulk = pl.pallas_call(
        lambda *refs: pack_body(bits, *refs),
        out_shape=[shape((KV_ROWS, W), BF16)] + [shape((BULK_ROWS, W), BF16)] * bits,
        in_specs=[hbm] * 5,
        out_specs=[vmem] * (1 + bits),
        scratch_shapes=[
            pltpu.VMEM((HEADS, W), F32),
            pltpu.VMEM((32, W), BF16),
            pltpu.SemaphoreType.DMA((3 + bits * (GROUPS + 8),)),
        ],
        compiler_params=params,
        name="pack",
    )(
        *(
            pltpu.with_memory_space_constraint(array, pltpu.HBM)
            for array in (mixer_input, step_input, mixer_cotangent, attn_keys, attn_values)
        )
    )

    def swap(array, k, keep=lambda i, j: True, axis="ctx"):
        pairs = [(i, i ^ k) for i in range(sizes[axis]) if keep(i, i ^ k)]
        return lax.ppermute(array, axis, pairs)

    nears = [swap(near, k, lambda i, j: j > i) for k in range(1, ctx)]
    bulks = [swap(bulk[k.bit_length() - 1], k) for k in range(1, ctx)]

    query_grad, own, *parts = pl.pallas_call(
        lambda *refs: attend_body(peers, *refs),
        out_shape=[shape(queries.shape, BF16), shape((KV_ROWS, W), F32)]
        + [shape((KV_ROWS, W), BF16)] * peers,
        in_specs=[vmem] * (4 + peers),
        out_specs=[vmem] * (2 + peers),
        compiler_params=params,
        name="attend",
    )(queries, attn_keys, attn_values, attn_cotangent, *nears)

    input_grad, step_grad, edge, first, pay = pl.pallas_call(
        lambda *refs: mixer_body(peers, *refs),
        out_shape=[
            shape(mixer_input.shape, BF16),
            shape(step_input.shape, F32),
            shape((16, GROUPS * W), F32),
            shape((8, GROUPS * W), F32),
            shape((PAY_ROWS, W), F32),
        ],
        in_specs=[vmem] * 3 + [smem] * 3 + [vmem] * (1 + peers),
        out_specs=[vmem] * 5,
        scratch_shapes=[
            pltpu.VMEM((ctx + 1, 16 * GROUPS, W), BF16),
            pltpu.VMEM((GROUPS, W + 8, W), F32),
            pltpu.VMEM((GROUPS, W + 8, W), F32),
            pltpu.VMEM((peers * GROUPS, W + 8, W), F32),
            pltpu.VMEM((HEADS, W, W), F32),
            pltpu.VMEM((HEADS, W, W), F32),
            pltpu.VMEM((GROUPS, W, W), F32),
            pltpu.VMEM((GROUPS, W, W), F32),
        ],
        compiler_params=params,
        name="mixer",
    )(mixer_input, step_input, conv_weight, decay_log, step_bias, residual, mixer_cotangent, *bulks)

    returned = [swap(parts[k - 1], k, lambda i, j: j < i) for k in range(1, ctx)]
    halo = lax.ppermute(first, "ctx", [(i + 1, i) for i in range(ctx - 1)])
    stages = [("dp", 1 << b) for b in range(dp.bit_length() - 1)]
    stages += [("ctx", 1 << b) for b in range(bits)]
    for n, (axis, k) in enumerate(stages):
        other = swap(pay, k, axis=axis)
        if n + 1 < len(stages):
            pay = pay + other

    blocks = mixer_input.shape[1] // 16
    last = pl.BlockSpec((1, 16, GROUPS * W), lambda i: (0, blocks - 1, 0))
    input_grad, key_grad, value_grad, conv_grad, decay_grad, bias_grad, skip_grad = pl.pallas_call(
        lambda *refs: finish_body(peers, dp, *refs),
        out_shape=[
            shape(mixer_input.shape, BF16),
            shape(attn_keys.shape, BF16),
            shape(attn_values.shape, BF16),
            shape(conv_weight.shape, F32),
        ]
        + [shape((HEADS,), F32)] * 3,
        grid=(1,),
        in_specs=[last] + [vmem] * (6 + peers),
        out_specs=[last] + [vmem] * 3 + [smem] * 3,
        input_output_aliases={0: 0},
        compiler_params=pltpu.CompilerParams(vmem_limit_bytes=LIMIT),
        name="finish",
    )(input_grad, edge, halo, conv_weight, own, pay, other, *returned)
    return (
        input_grad,
        jnp.swapaxes(step_grad, 1, 2),
        conv_grad,
        decay_grad,
        bias_grad,
        skip_grad,
        query_grad,
        key_grad,
        value_grad,
    )


def solution(mesh):
    split = P("dp", "ctx", None)
    sizes = dict(mesh.shape)

    def step(*args):
        return on_device(sizes, *args)

    return jax.shard_map(
        step,
        mesh=mesh,
        in_specs=(split, split, P(), P(), P(), P(), split, split, split, split, split),
        out_specs=(split, split, P(), P(), P(), P(), split, split, split),
        check_vma=False,
    )
```

```python
import jax
import jax.numpy as jnp
from jax import lax
from jax.experimental import pallas as pl
from jax.experimental.pallas import tpu as pltpu
from jax.sharding import PartitionSpec as P


F32 = jnp.float32
BF16 = jnp.bfloat16
HEADS = 4
TAPS = 4
W = 128
GROUPS = HEADS + 2
KV_ROWS = 2 * W
NEAR_ROWS = KV_ROWS + 32
STEP_ROW = (HEADS + 1) * W
EDGE_ROW = STEP_ROW + 16
BULK_ROWS = EDGE_ROW + 16
PAY_ROWS = 40
LIMIT = 16 << 20
LOG2E = 1.4426950408889634


def dot(a, b, dims=((1,), (0,)), precise=False):
    return lax.dot_general(
        a,
        b,
        (dims, ((), ())),
        precision=lax.Precision.HIGHEST if precise else None,
        preferred_element_type=F32,
    )


def split(array):
    high = array.astype(BF16)
    return high, (array - high.astype(F32)).astype(BF16)


def dot_split(a, b, dims=((1,), (0,))):
    a = a if isinstance(a, tuple) else (a,)
    b = b if isinstance(b, tuple) else (b,)
    total = dot(a[0], b[0], dims)
    if len(a) > 1:
        total = total + dot(a[1], b[0], dims)
    if len(b) > 1:
        total = total + dot(a[0], b[1], dims)
    return total


NT = ((1,), (1,))
TN = ((0,), (0,))


def iota2(dim):
    return lax.broadcasted_iota(jnp.int32, (W, W), dim)


def cols(g):
    return slice(g * W, (g + 1) * W)


def small_rows(rows):
    rows = rows + [jnp.zeros((32 - 3 * GROUPS, W), F32)]
    return jnp.concatenate(rows, axis=0).astype(BF16)


def pack_body(bits, mixer, step, cotan, keys, values, near, *refs):
    bulk, (size, extra, sems) = refs[:bits], refs[bits:]
    me = lax.axis_index("ctx")

    def copy(source, target, at):
        return pltpu.make_async_copy(source, target, sems.at[at])

    first = [
        copy(step.at[0], size, 0),
        copy(keys.at[0], near.at[0:W, :], 1),
        copy(values.at[0], near.at[W : 2 * W, :], 2),
    ]
    for c in first:
        c.start()
    later = [jnp.bitwise_and(lax.shift_right_logical(me, b), 1) == 0 for b in range(bits)]
    forward, backward = [], []
    for b in range(bits):
        at = 3 + b * (GROUPS + 6)
        forward.append(
            [
                copy(mixer.at[0, :, cols(g)], bulk[b].at[cols(g), :], at + g)
                for g in range(HEADS + 1)
            ]
            + [
                copy(
                    mixer.at[0, W - 16 : W, cols(HEADS + 1)],
                    bulk[b].at[EDGE_ROW:BULK_ROWS, :],
                    at + HEADS + 1,
                )
            ]
        )
        backward.append(
            [
                copy(cotan.at[0, :, cols(g)], bulk[b].at[cols(g), :], at + GROUPS + g)
                for g in range(HEADS)
            ]
            + [
                copy(
                    mixer.at[0, :, cols(HEADS + 1)],
                    bulk[b].at[cols(HEADS), :],
                    at + GROUPS + HEADS,
                )
            ]
        )

        @pl.when(later[b])
        def _(b=b):
            for c in forward[b]:
                c.start()

        @pl.when(jnp.logical_not(later[b]))
        def _(b=b):
            for c in backward[b]:
                c.start()

    for c in first:
        c.wait()
    rows = size[...]
    high = rows.astype(BF16).astype(F32)
    mid = (rows - high).astype(BF16).astype(F32)
    low = rows - high - mid
    extra[0:16, :] = jnp.concatenate([high, mid, low, jnp.zeros_like(low)], axis=0).astype(BF16)
    extra[16:32, :] = jnp.zeros((16, W), BF16)
    for b in range(bits):
        at = 3 + bits * (GROUPS + 6) + 2 * b
        sized = copy(extra.at[0:16, :], bulk[b].at[STEP_ROW:EDGE_ROW, :], at)
        empty = copy(extra.at[16:32, :], bulk[b].at[EDGE_ROW:BULK_ROWS, :], at + 1)
        forward[b].append(sized)
        backward[b] += [sized, empty]
        sized.start()

        @pl.when(later[b])
        def _(b=b):
            for c in forward[b]:
                c.wait()

        @pl.when(jnp.logical_not(later[b]))
        def _(b=b, empty=empty):
            empty.start()
            for c in backward[b]:
                c.wait()


def attend_heads(peers, heads, queries, keys, values, cotan, near, query_grad, sums):
    me = lax.axis_index("ctx")
    scale = W ** (-0.5)
    keys_all = jnp.concatenate([keys[0]] + [m[0:W, :] for m in near], axis=0)
    values_all = jnp.concatenate([values[0]] + [m[W : 2 * W, :] for m in near], axis=0)
    causal = iota2(0) >= iota2(1)
    rounded_heads, dscore_heads = [], []
    for r in heads:
        query = queries[0, :, cols(r)]
        cot = cotan[0, :, cols(r)]
        scores = dot(query, keys_all, NT) * (scale * LOG2E)
        blocks = [jnp.where(causal, scores[:, 0:W], -jnp.inf)]
        for k in range(1, peers + 1):
            bit = k.bit_length() - 1
            earlier = jnp.bitwise_and(lax.shift_right_logical(me, bit), 1) == 1
            blocks.append(jnp.where(earlier, scores[:, cols(k)], -jnp.inf))
        scores = jnp.concatenate(blocks, axis=1)
        top = jnp.max(scores, axis=1, keepdims=True)
        weights = jnp.exp2(scores - top)
        probs = weights * (1.0 / jnp.sum(weights, axis=1, keepdims=True))
        rounded = probs.astype(BF16)
        attended = dot(rounded, values_all)
        delta = jnp.sum(cot.astype(F32) * attended, axis=1, keepdims=True)
        dprob = dot(cot, values_all, NT)
        dscore = (probs * (dprob - delta) * scale).astype(BF16)
        query_grad[0, :, cols(r)] = dot(dscore, keys_all).astype(BF16)
        rounded_heads.append(rounded)
        dscore_heads.append(dscore)
    query_rows = jnp.concatenate([queries[0, :, cols(r)] for r in heads], axis=0)
    cotan_rows = jnp.concatenate([cotan[0, :, cols(r)] for r in heads], axis=0)
    key_acc = dot(jnp.concatenate(dscore_heads, axis=0), query_rows, TN)
    value_acc = dot(jnp.concatenate(rounded_heads, axis=0), cotan_rows, TN)
    if sums is not None:
        key_acc, value_acc = key_acc + sums[0], value_acc + sums[1]
    return key_acc, value_acc


def half_body(peers, *refs):
    near = refs[4 : 4 + peers]
    query_grad, sums = refs[4 + peers :]
    sums[0], sums[1] = attend_heads(peers, range(HEADS // 2), *refs[:4], near, query_grad, None)


def attend_body(peers, *refs):
    near = refs[4 : 4 + peers]
    half, sums, halo, query_grad, own, *parts = refs[4 + peers :]
    query_grad[0, :, 0 : HEADS // 2 * W] = half[0]
    key_acc, value_acc = attend_heads(
        peers, range(HEADS // 2, HEADS), *refs[:4], near, query_grad, sums
    )
    own[0:W, :] = key_acc[0:W]
    own[W : 2 * W, :] = value_acc[0:W]
    for k in range(1, peers + 1):
        parts[k - 1][0:W, :] = key_acc[cols(k)].astype(BF16)
        parts[k - 1][W : 2 * W, :] = value_acc[cols(k)].astype(BF16)
        parts[k - 1][KV_ROWS:NEAR_ROWS, :] = halo[...]


def head_column(ref, lanes):
    return jnp.concatenate([jnp.full((1, lanes), ref[h], F32) for h in range(HEADS)], axis=0)


def sigmoid(v):
    return 0.5 * jnp.tanh(0.5 * v) + 0.5


def mixer_body(peers, *refs):
    mixer, step, weight, decay_log, bias, residual, cotan = refs[:7]
    bulk = refs[7 : 7 + peers]
    input_grad, step_grad, edge, halo, pay = refs[7 + peers : 12 + peers]
    tails, ext, grads, peer_ext, states, adjoints, acts, slopes = refs[12 + peers :]
    me = lax.axis_index("ctx")
    slots = peers + 1
    index = [me] + [jnp.bitwise_xor(me, k) for k in range(1, slots)]

    tails[0] = jnp.zeros((16 * GROUPS, W), BF16)
    for g in range(GROUPS):
        tails[me + 1, 16 * g : 16 * g + 16, :] = mixer[0, W - 16 : W, cols(g)]
    for k in range(1, slots):
        earlier = index[k] < me

        @pl.when(earlier)
        def _(k=k):
            for g in range(HEADS + 1):
                tails[index[k] + 1, 16 * g : 16 * g + 16, :] = bulk[k - 1][
                    (g + 1) * W - 16 : (g + 1) * W, :
                ]
            tails[index[k] + 1, 16 * (GROUPS - 1) : 16 * GROUPS, :] = bulk[k - 1][
                EDGE_ROW:BULK_ROWS, :
            ]

        @pl.when(jnp.logical_not(earlier))
        def _(k=k):
            tails[index[k] + 1, 16 * (GROUPS - 1) : 16 * GROUPS, :] = bulk[k - 1][
                STEP_ROW - 16 : STEP_ROW, :
            ]

    pieces = [step[0]]
    for k in range(1, slots):
        sent = bulk[k - 1][STEP_ROW:EDGE_ROW, :].astype(F32)
        pieces.append(sent[0:4] + sent[4:8] + sent[8:12])
    rate = -jnp.exp(head_column(decay_log, W))
    raw = jnp.concatenate(pieces, axis=0) + jnp.concatenate([head_column(bias, W)] * slots, axis=0)
    sizes = jnp.maximum(raw, 0.0) + jnp.log(1.0 + jnp.exp(-jnp.abs(raw)))
    decays = sizes * jnp.concatenate([rate] * slots, axis=0)
    upto = (iota2(0) <= iota2(1)).astype(F32)
    cumulative = dot(decays, upto, precise=True)

    def rows_of(array, k):
        return array[HEADS * k : HEADS * (k + 1)]

    totals = [
        jnp.broadcast_to(rows_of(cumulative, k)[:, W - 1 : W], (HEADS, W)) for k in range(slots)
    ]
    own_cum = rows_of(cumulative, 0)
    own_size = rows_of(sizes, 0)
    table = [own_cum, own_size, jnp.exp(own_cum), jnp.exp(totals[0] - own_cum)]
    for k in range(1, slots):
        low, high = jnp.minimum(me, index[k]), jnp.maximum(me, index[k])
        between = jnp.zeros((HEADS, W), F32)
        for m in range(1, slots):
            inside = jnp.logical_and(index[m] > low, index[m] < high)
            between = between + jnp.where(inside, totals[m], 0.0)
        earlier = index[k] < me
        cum = rows_of(cumulative, k)
        span = jnp.where(earlier, totals[k] - cum, cum) + between
        table.append(jnp.exp(span) * jnp.where(earlier, rows_of(sizes, k), 1.0))
    table.append(jnp.zeros((W - HEADS * len(table), W), F32))
    columns = jnp.transpose(jnp.concatenate(table, axis=0))

    def column(group, h):
        at = HEADS * group + h
        return columns[:, at : at + 1]

    def convolve(place, g):
        total = place[5 : 5 + W, :] * weight[0:1, cols(g)]
        for offset in range(1, TAPS):
            total = total + place[5 + offset : 5 + offset + W, :] * weight[offset : offset + 1, cols(g)]
        return total

    def peer_act(k, at, g):
        place = peer_ext.at[(k - 1) * GROUPS + g]
        place[0:8, :] = tails[index[k], 16 * g : 16 * g + 16, :].astype(F32)[8:16]
        place[8 : 8 + W, :] = bulk[k - 1][cols(at), :].astype(F32)
        pre = convolve(place, g)
        return pre * sigmoid(pre)

    states[...] = jnp.zeros_like(states)
    adjoints[...] = jnp.zeros_like(adjoints)
    for k in range(1, slots):
        earlier = index[k] < me

        @pl.when(earlier)
        def _(k=k):
            map_in = split(peer_act(k, HEADS, HEADS))
            for h in range(HEADS):
                rows = split(peer_act(k, h, h) * column(3 + k, h))
                states[h] = states[h] + dot_split(rows, map_in, TN)

        @pl.when(jnp.logical_not(earlier))
        def _(k=k):
            map_out = peer_act(k, HEADS, HEADS + 1)
            for h in range(HEADS):
                read = split(map_out * column(3 + k, h))
                adjoints[h] = adjoints[h] + dot_split(bulk[k - 1][cols(h), :], read, TN)

    for g in range(GROUPS):
        place = ext.at[g]
        place[0:8, :] = tails[me, 16 * g : 16 * g + 16, :].astype(F32)[8:16]
        place[8 : 8 + W, :] = mixer[0, :, cols(g)].astype(F32)
        pre = convolve(place, g)
        sig = sigmoid(pre)
        acts[g] = pre * sig
        slopes[g] = sig + pre * sig * (1.0 - sig)

    map_in, map_out = acts[HEADS], acts[HEADS + 1]
    map_in_s, map_out_s = split(map_in), split(map_out)
    map_in_b, map_out_b = map_in_s[0], map_out_s[0]
    meets = dot_split(map_out_s, map_in_s, NT)
    lower = iota2(0) >= iota2(1)
    ones = jnp.ones((16, W), BF16)
    grad_in = jnp.zeros((W, W), F32)
    grad_out = jnp.zeros((W, W), F32)
    grad_meets = jnp.zeros((W, W), F32)
    flow_rows, tail_rows, size_rows, pass_rows, skip_rows = [], [], [], [], []
    for h in range(HEADS):
        cot_b = cotan[0, :, cols(h)]
        cot = cot_b.astype(F32)
        act = acts[h]
        size = column(1, h)
        tail = column(3, h)
        scaled = act * size
        state = states[h]
        adjoint = adjoints[h]
        adjoint_s = split(adjoint)
        falloff = jnp.where(lower, jnp.exp(column(0, h) - own_cum[h : h + 1]), 0.0)
        pair = dot_split(cot_b, split(scaled), NT) * falloff
        grad_meets = grad_meets + pair
        flow = split(pair * meets)
        projected = tail * dot_split(map_in_s, adjoint_s, NT)
        mixed = dot_split(split(falloff * meets), cot_b, TN)
        grad_scaled = mixed + projected
        lead_read = column(2, h) * dot_split(cot_b, split(state))
        grad_out = grad_out + lead_read
        grad_in = grad_in + dot((scaled * tail).astype(BF16), adjoint_s[0])
        carried = split(lead_read * map_out)
        trailing = split(projected * act)
        sized = split(mixed * act)
        flow_rows.append(
            (dot_split(ones, flow, NT) - dot_split(ones, flow) + dot_split(ones, carried, NT))[0:1]
        )
        trail = dot_split(ones, trailing, NT)[0:1]
        tail_rows.append(trail * own_size[h : h + 1])
        size_rows.append(dot_split(ones, sized, NT)[0:1] + trail)
        passed = jnp.sum(jnp.sum(state * adjoint, axis=0, keepdims=True), axis=1, keepdims=True)
        pass_rows.append(jnp.broadcast_to(passed, (1, W)))
        skip_rows.append(jnp.sum(cot * act, axis=0, keepdims=True))
        grads[h, 0:W, :] = (residual[h] * cot + grad_scaled * size) * slopes[h]
    grad_meets_b = grad_meets.astype(BF16)
    grad_out = grad_out + dot(grad_meets_b, map_in_b)
    grad_in = grad_in + dot(grad_meets_b, map_out_b, TN)
    grads[HEADS, 0:W, :] = grad_in * slopes[HEADS]
    grads[HEADS + 1, 0:W, :] = grad_out * slopes[HEADS + 1]

    since = (iota2(0) >= iota2(1)).astype(F32)
    before = (iota2(0) < iota2(1)).astype(F32)
    grad_decay = (
        dot(jnp.concatenate(flow_rows, axis=0), since, precise=True)
        + dot(jnp.concatenate(tail_rows, axis=0), before, precise=True)
        + jnp.exp(totals[0]) * jnp.concatenate(pass_rows, axis=0)
    )
    grad_step = grad_decay * rate + jnp.concatenate(size_rows, axis=0)
    grad_raw = grad_step * sigmoid(rows_of(raw, 0))
    step_grad[0] = grad_raw
    pay[24:28, :] = grad_decay * own_size * rate
    pay[28:32, :] = grad_raw
    pay[32:36, :] = jnp.concatenate(skip_rows, axis=0)
    pay[36:40, :] = jnp.zeros((4, W), F32)

    halo[...] = small_rows([grads[g, 0:8, :][0:3] for g in range(GROUPS)])
    for g in range(GROUPS):
        grads[g, W : W + 8, :] = jnp.zeros((8, W), F32)
        grad = grads[g, 0:W, :]
        total = grads[g, TAPS - 1 : TAPS - 1 + W, :] * weight[0:1, cols(g)]
        for offset in range(1, TAPS):
            at = TAPS - 1 - offset
            total = total + grads[g, at : at + W, :] * weight[offset : offset + 1, cols(g)]
        input_grad[0, :, cols(g)] = total.astype(BF16)
        edge[:, cols(g)] = total[W - 16 : W]
        for offset in range(TAPS):
            pay[4 * g + offset : 4 * g + offset + 1, :] = jnp.sum(
                grad * ext[g, 5 + offset : 5 + offset + W, :], axis=0, keepdims=True
            )


def finish_body(peers, *refs):
    partial, edge, weight, own = refs[:4]
    parts = refs[4 : 4 + peers]
    input_grad, key_grad, value_grad = refs[4 + peers :]
    me = lax.axis_index("ctx")
    both = own[...]
    halo = jnp.zeros((32, W), F32)
    for k in range(1, peers + 1):
        both = both + parts[k - 1][0:KV_ROWS, :].astype(F32)
        after = jnp.bitwise_xor(me, k) == me + 1
        halo = halo + jnp.where(after, parts[k - 1][KV_ROWS:NEAR_ROWS, :].astype(F32), 0.0)
    key_grad[0] = both[0:W].astype(BF16)
    value_grad[0] = both[W : 2 * W].astype(BF16)
    row = lax.broadcasted_iota(jnp.int32, (16, W), 0)
    for g in range(GROUPS):
        rows = edge[:, cols(g)]
        for offset in range(TAPS - 1):
            for t in range(TAPS - 1 - offset):
                at = 16 - (TAPS - 1 - offset) + t
                piece = halo[3 * g + t : 3 * g + t + 1] * weight[offset : offset + 1, cols(g)]
                rows = rows + jnp.where(row == at, piece, 0.0)
        input_grad[0, 0 : W - 16, cols(g)] = partial[0, 0 : W - 16, cols(g)]
        input_grad[0, W - 16 : W, cols(g)] = rows.astype(BF16)


def total_body(count, total_a, total_b, conv_grad, decay_grad, bias_grad, skip_grad):
    total = (total_a[...] + total_b[...]) * (1.0 / count)
    for g in range(GROUPS):
        conv_grad[:, cols(g)] = total[4 * g : 4 * g + 4]
    sums = jnp.sum(total[24:40], axis=1, keepdims=True)
    for h in range(HEADS):
        decay_grad[h] = jnp.sum(sums[h : h + 1])
        bias_grad[h] = jnp.sum(sums[4 + h : 5 + h])
        skip_grad[h] = jnp.sum(sums[8 + h : 9 + h])


def shape(dims, dtype):
    return jax.ShapeDtypeStruct(dims, dtype)


def on_device(sizes, *args):
    (
        mixer_input,
        step_input,
        conv_weight,
        decay_log,
        step_bias,
        residual,
        mixer_cotangent,
        queries,
        attn_keys,
        attn_values,
        attn_cotangent,
    ) = args
    ctx, dp = sizes["ctx"], sizes["dp"]
    step_input = jnp.swapaxes(step_input, 1, 2)
    peers = ctx - 1
    bits = ctx.bit_length() - 1
    vmem = pl.BlockSpec(memory_space=pltpu.VMEM)
    smem = pl.BlockSpec(memory_space=pltpu.SMEM)

    hbm = pl.BlockSpec(memory_space=pltpu.HBM)
    params = pltpu.CompilerParams(vmem_limit_bytes=LIMIT)
    near, *bulk = pl.pallas_call(
        lambda *refs: pack_body(bits, *refs),
        out_shape=[shape((KV_ROWS, W), BF16)] + [shape((BULK_ROWS, W), BF16)] * bits,
        in_specs=[hbm] * 5,
        out_specs=[vmem] * (1 + bits),
        scratch_shapes=[
            pltpu.VMEM((HEADS, W), F32),
            pltpu.VMEM((32, W), BF16),
            pltpu.SemaphoreType.DMA((3 + bits * (GROUPS + 8),)),
        ],
        compiler_params=params,
        name="pack",
    )(
        *(
            pltpu.with_memory_space_constraint(array, pltpu.HBM)
            for array in (mixer_input, step_input, mixer_cotangent, attn_keys, attn_values)
        )
    )

    def swap(array, k, keep=lambda i, j: True, axis="ctx"):
        pairs = [(i, i ^ k) for i in range(sizes[axis]) if keep(i, i ^ k)]
        return lax.ppermute(array, axis, pairs)

    nears = [swap(near, k, lambda i, j: j > i) for k in range(1, ctx)]
    bulks = [swap(bulk[k.bit_length() - 1], k) for k in range(1, ctx)]

    input_grad, step_grad, edge, halo, pay = pl.pallas_call(
        lambda *refs: mixer_body(peers, *refs),
        out_shape=[
            shape(mixer_input.shape, BF16),
            shape(step_input.shape, F32),
            shape((16, GROUPS * W), F32),
            shape((32, W), BF16),
            shape((PAY_ROWS, W), F32),
        ],
        in_specs=[vmem] * 3 + [smem] * 3 + [vmem] * (1 + peers),
        out_specs=[vmem] * 5,
        scratch_shapes=[
            pltpu.VMEM((ctx + 1, 16 * GROUPS, W), BF16),
            pltpu.VMEM((GROUPS, W + 8, W), F32),
            pltpu.VMEM((GROUPS, W + 8, W), F32),
            pltpu.VMEM((peers * GROUPS, W + 8, W), F32),
            pltpu.VMEM((HEADS, W, W), F32),
            pltpu.VMEM((HEADS, W, W), F32),
            pltpu.VMEM((GROUPS, W, W), F32),
            pltpu.VMEM((GROUPS, W, W), F32),
        ],
        compiler_params=params,
        name="mixer",
    )(mixer_input, step_input, conv_weight, decay_log, step_bias, residual, mixer_cotangent, *bulks)

    half, sums = pl.pallas_call(
        lambda *refs: half_body(peers, *refs),
        out_shape=[
            shape((1, W, HEADS // 2 * W), BF16),
            shape((2, ctx * W, W), F32),
        ],
        in_specs=[vmem] * (4 + peers),
        out_specs=[vmem] * 2,
        compiler_params=params,
        name="half",
    )(queries, attn_keys, attn_values, attn_cotangent, *nears)

    query_grad, own, *parts = pl.pallas_call(
        lambda *refs: attend_body(peers, *refs),
        out_shape=[shape(queries.shape, BF16), shape((KV_ROWS, W), F32)]
        + [shape((NEAR_ROWS, W), BF16)] * peers,
        in_specs=[vmem] * (7 + peers),
        out_specs=[vmem] * (2 + peers),
        compiler_params=params,
        name="attend",
    )(queries, attn_keys, attn_values, attn_cotangent, *nears, half, sums, halo)

    returned = [swap(parts[k - 1], k, lambda i, j: j < i) for k in range(1, ctx)]
    stages = [("dp", 1 << b) for b in range(dp.bit_length() - 1)]
    stages += [("ctx", 1 << b) for b in range(bits)]
    for n, (axis, k) in enumerate(stages):
        other = swap(pay, k, axis=axis)
        if n + 1 < len(stages):
            pay = pay + other

    input_grad, key_grad, value_grad = pl.pallas_call(
        lambda *refs: finish_body(peers, *refs),
        out_shape=[
            shape(mixer_input.shape, BF16),
            shape(attn_keys.shape, BF16),
            shape(attn_values.shape, BF16),
        ],
        in_specs=[vmem] * (4 + peers),
        out_specs=[vmem] * 3,
        compiler_params=params,
        name="finish",
    )(input_grad, edge, conv_weight, own, *returned)
    conv_grad, decay_grad, bias_grad, skip_grad = pl.pallas_call(
        lambda *refs: total_body(dp, *refs),
        out_shape=[shape(conv_weight.shape, F32)] + [shape((HEADS,), F32)] * 3,
        in_specs=[vmem] * 2,
        out_specs=[vmem] + [smem] * 3,
        compiler_params=params,
        name="total",
    )(pay, other)
    return (
        input_grad,
        jnp.swapaxes(step_grad, 1, 2),
        conv_grad,
        decay_grad,
        bias_grad,
        skip_grad,
        query_grad,
        key_grad,
        value_grad,
    )


def solution(mesh):
    split = P("dp", "ctx", None)
    sizes = dict(mesh.shape)

    def step(*args):
        return on_device(sizes, *args)

    return jax.shard_map(
        step,
        mesh=mesh,
        in_specs=(split, split, P(), P(), P(), P(), split, split, split, split, split),
        out_specs=(split, split, P(), P(), P(), P(), split, split, split),
        check_vma=False,
    )
```

```python
import jax
import jax.numpy as jnp
from jax import lax
from jax.experimental import pallas as pl
from jax.experimental.pallas import tpu as pltpu
from jax.sharding import PartitionSpec as P


F32 = jnp.float32
BF16 = jnp.bfloat16
HEADS = 4
TAPS = 4
W = 128
GROUPS = HEADS + 2
KV_ROWS = 2 * W
SUM_ROW = KV_ROWS + 32
MIX_ROWS = SUM_ROW + 128
STEP_ROW = (HEADS + 1) * W
BULK_ROWS = STEP_ROW + 16
PAY_ROWS = 40
LIMIT = 16 << 20
LOG2E = 1.4426950408889634


def dot(a, b, dims=((1,), (0,)), precise=False):
    return lax.dot_general(
        a,
        b,
        (dims, ((), ())),
        precision=lax.Precision.HIGHEST if precise else None,
        preferred_element_type=F32,
    )


def split(array):
    high = array.astype(BF16)
    return high, (array - high.astype(F32)).astype(BF16)


def dot_split(a, b, dims=((1,), (0,))):
    a = a if isinstance(a, tuple) else (a,)
    b = b if isinstance(b, tuple) else (b,)
    total = dot(a[0], b[0], dims)
    if len(a) > 1:
        total = total + dot(a[1], b[0], dims)
    if len(b) > 1:
        total = total + dot(a[0], b[1], dims)
    return total


NT = ((1,), (1,))
TN = ((0,), (0,))


def iota2(dim):
    return lax.broadcasted_iota(jnp.int32, (W, W), dim)


def cols(g):
    return slice(g * W, (g + 1) * W)


def small_rows(rows):
    rows = rows + [jnp.zeros((32 - 3 * GROUPS, W), F32)]
    return jnp.concatenate(rows, axis=0).astype(BF16)


def in_pieces(rows, count):
    high = rows.astype(BF16).astype(F32)
    mid = (rows - high).astype(BF16).astype(F32)
    low = rows - high - mid
    parts = [high, mid, low]
    if count > 3 * rows.shape[0]:
        parts.append(jnp.zeros((count - 3 * rows.shape[0], W), F32))
    return jnp.concatenate(parts, axis=0).astype(BF16)


def pack_body(bits, mixer, step, cotan, keys, values, near, *refs):
    bulk, (size, ends, extra, sems) = refs[:bits], refs[bits:]
    me = lax.axis_index("ctx")

    def copy(source, target, at):
        return pltpu.make_async_copy(source, target, sems.at[at])

    first = [
        copy(step.at[0], size, 0),
        copy(keys.at[0], near.at[0:W, :], 1),
        copy(values.at[0], near.at[W : 2 * W, :], 2),
        copy(mixer.at[0, W - 16 : W, cols(HEADS + 1)], ends, 3),
    ]
    for c in first:
        c.start()
    later = [jnp.bitwise_and(lax.shift_right_logical(me, b), 1) == 0 for b in range(bits)]
    forward, backward = [], []
    for b in range(bits):
        at = 4 + b * (GROUPS + 6)
        forward.append(
            [
                copy(mixer.at[0, :, cols(g)], bulk[b].at[cols(g), :], at + g)
                for g in range(HEADS + 1)
            ]
        )
        backward.append(
            [
                copy(cotan.at[0, :, cols(g)], bulk[b].at[cols(g), :], at + GROUPS + g)
                for g in range(HEADS)
            ]
            + [
                copy(
                    mixer.at[0, :, cols(HEADS + 1)],
                    bulk[b].at[cols(HEADS), :],
                    at + GROUPS + HEADS,
                )
            ]
        )

        @pl.when(later[b])
        def _(b=b):
            for c in forward[b]:
                c.start()

        @pl.when(jnp.logical_not(later[b]))
        def _(b=b):
            for c in backward[b]:
                c.start()

    for c in first:
        c.wait()
    pieces = in_pieces(size[...], 12).astype(F32)
    last = ends[...].astype(F32)[12:16]
    extra[...] = jnp.concatenate([pieces, last], axis=0).astype(BF16)
    for b in range(bits):
        at = 4 + bits * (GROUPS + 6) + b
        sized = copy(extra, bulk[b].at[STEP_ROW:BULK_ROWS, :], at)
        forward[b].append(sized)
        backward[b].append(sized)
        sized.start()

        @pl.when(later[b])
        def _(b=b):
            for c in forward[b]:
                c.wait()

        @pl.when(jnp.logical_not(later[b]))
        def _(b=b):
            for c in backward[b]:
                c.wait()


def attend_heads(peers, heads, queries, keys, values, cotan, near, query_grad, sums):
    me = lax.axis_index("ctx")
    scale = W ** (-0.5)
    keys_all = jnp.concatenate([keys[0]] + [m[0:W, :] for m in near], axis=0)
    values_all = jnp.concatenate([values[0]] + [m[W : 2 * W, :] for m in near], axis=0)
    causal = iota2(0) >= iota2(1)
    rounded_heads, dscore_heads = [], []
    for r in heads:
        query = queries[0, :, cols(r)]
        cot = cotan[0, :, cols(r)]
        scores = dot(query, keys_all, NT) * (scale * LOG2E)
        blocks = [jnp.where(causal, scores[:, 0:W], -jnp.inf)]
        for k in range(1, peers + 1):
            bit = k.bit_length() - 1
            earlier = jnp.bitwise_and(lax.shift_right_logical(me, bit), 1) == 1
            blocks.append(jnp.where(earlier, scores[:, cols(k)], -jnp.inf))
        scores = jnp.concatenate(blocks, axis=1)
        top = jnp.max(scores, axis=1, keepdims=True)
        weights = jnp.exp2(scores - top)
        probs = weights * (1.0 / jnp.sum(weights, axis=1, keepdims=True))
        rounded = probs.astype(BF16)
        attended = dot(rounded, values_all)
        delta = jnp.sum(cot.astype(F32) * attended, axis=1, keepdims=True)
        dprob = dot(cot, values_all, NT)
        dscore = (probs * (dprob - delta) * scale).astype(BF16)
        query_grad[0, :, cols(r)] = dot(dscore, keys_all).astype(BF16)
        rounded_heads.append(rounded)
        dscore_heads.append(dscore)
    query_rows = jnp.concatenate([queries[0, :, cols(r)] for r in heads], axis=0)
    cotan_rows = jnp.concatenate([cotan[0, :, cols(r)] for r in heads], axis=0)
    key_acc = dot(jnp.concatenate(dscore_heads, axis=0), query_rows, TN)
    value_acc = dot(jnp.concatenate(rounded_heads, axis=0), cotan_rows, TN)
    if sums is not None:
        key_acc, value_acc = key_acc + sums[0], value_acc + sums[1]
    return key_acc, value_acc


def half_body(peers, *refs):
    near = refs[4 : 4 + peers]
    query_grad, sums = refs[4 + peers :]
    sums[0], sums[1] = attend_heads(peers, range(HEADS // 2), *refs[:4], near, query_grad, None)


def attend_body(peers, *refs):
    near = refs[4 : 4 + peers]
    half, sums, query_grad, own, *parts = refs[4 + peers :]
    query_grad[0, :, 0 : HEADS // 2 * W] = half[0]
    key_acc, value_acc = attend_heads(
        peers, range(HEADS // 2, HEADS), *refs[:4], near, query_grad, sums
    )
    own[0:W, :] = key_acc[0:W]
    own[W : 2 * W, :] = value_acc[0:W]
    for k in range(1, peers + 1):
        parts[k - 1][0:W, :] = key_acc[cols(k)].astype(BF16)
        parts[k - 1][W : 2 * W, :] = value_acc[cols(k)].astype(BF16)


def head_column(ref, lanes):
    return jnp.concatenate([jnp.full((1, lanes), ref[h], F32) for h in range(HEADS)], axis=0)


def sigmoid(v):
    return 0.5 * jnp.tanh(0.5 * v) + 0.5


def mixer_body(peers, *refs):
    mixer, step, weight, decay_log, bias, residual, cotan = refs[:7]
    bulk = refs[7 : 7 + peers]
    step_grad, grads, halo, pay = refs[7 + peers : 11 + peers]
    tails, ext, peer_ext, states, adjoints, acts, slopes = refs[11 + peers :]
    me = lax.axis_index("ctx")
    slots = peers + 1
    index = [me] + [jnp.bitwise_xor(me, k) for k in range(1, slots)]

    tails[0] = jnp.zeros((16 * GROUPS, W), BF16)
    for g in range(GROUPS):
        tails[me + 1, 16 * g : 16 * g + 16, :] = mixer[0, W - 16 : W, cols(g)]
    for k in range(1, slots):
        earlier = index[k] < me

        @pl.when(earlier)
        def _(k=k):
            for g in range(HEADS + 1):
                tails[index[k] + 1, 16 * g : 16 * g + 16, :] = bulk[k - 1][
                    (g + 1) * W - 16 : (g + 1) * W, :
                ]
            tails[index[k] + 1, 16 * (GROUPS - 1) : 16 * GROUPS, :] = bulk[k - 1][
                STEP_ROW:BULK_ROWS, :
            ]

        @pl.when(jnp.logical_not(earlier))
        def _(k=k):
            tails[index[k] + 1, 16 * (GROUPS - 1) : 16 * GROUPS, :] = bulk[k - 1][
                STEP_ROW - 16 : STEP_ROW, :
            ]

    pieces = [step[0]]
    for k in range(1, slots):
        sent = bulk[k - 1][STEP_ROW:BULK_ROWS, :].astype(F32)
        pieces.append(sent[0:4] + sent[4:8] + sent[8:12])
    rate = -jnp.exp(head_column(decay_log, W))
    raw = jnp.concatenate(pieces, axis=0) + jnp.concatenate([head_column(bias, W)] * slots, axis=0)
    sizes = jnp.maximum(raw, 0.0) + jnp.log(1.0 + jnp.exp(-jnp.abs(raw)))
    decays = sizes * jnp.concatenate([rate] * slots, axis=0)
    upto = (iota2(0) <= iota2(1)).astype(F32)
    cumulative = dot(decays, upto, precise=True)

    def rows_of(array, k):
        return array[HEADS * k : HEADS * (k + 1)]

    totals = [
        jnp.broadcast_to(rows_of(cumulative, k)[:, W - 1 : W], (HEADS, W)) for k in range(slots)
    ]
    own_cum = rows_of(cumulative, 0)
    own_size = rows_of(sizes, 0)
    table = [own_cum, own_size, jnp.exp(own_cum), jnp.exp(totals[0] - own_cum)]
    for k in range(1, slots):
        low, high = jnp.minimum(me, index[k]), jnp.maximum(me, index[k])
        between = jnp.zeros((HEADS, W), F32)
        for m in range(1, slots):
            inside = jnp.logical_and(index[m] > low, index[m] < high)
            between = between + jnp.where(inside, totals[m], 0.0)
        earlier = index[k] < me
        cum = rows_of(cumulative, k)
        span = jnp.where(earlier, totals[k] - cum, cum) + between
        table.append(jnp.exp(span) * jnp.where(earlier, rows_of(sizes, k), 1.0))
    table.append(jnp.zeros((W - HEADS * len(table), W), F32))
    columns = jnp.transpose(jnp.concatenate(table, axis=0))

    def column(group, h):
        at = HEADS * group + h
        return columns[:, at : at + 1]

    def convolve(place, g):
        total = place[5 : 5 + W, :] * weight[0:1, cols(g)]
        for offset in range(1, TAPS):
            total = total + place[5 + offset : 5 + offset + W, :] * weight[offset : offset + 1, cols(g)]
        return total

    def peer_act(k, at, g):
        place = peer_ext.at[(k - 1) * GROUPS + g]
        place[0:8, :] = tails[index[k], 16 * g : 16 * g + 16, :].astype(F32)[8:16]
        place[8 : 8 + W, :] = bulk[k - 1][cols(at), :].astype(F32)
        pre = convolve(place, g)
        return pre * sigmoid(pre)

    states[...] = jnp.zeros_like(states)
    adjoints[...] = jnp.zeros_like(adjoints)
    for k in range(1, slots):
        earlier = index[k] < me

        @pl.when(earlier)
        def _(k=k):
            map_in = split(jnp.transpose(peer_act(k, HEADS, HEADS)))
            for h in range(HEADS):
                rows = split(peer_act(k, h, h) * column(3 + k, h))
                states[h] = states[h] + dot_split(map_in, rows)

        @pl.when(jnp.logical_not(earlier))
        def _(k=k):
            map_out = jnp.transpose(peer_act(k, HEADS, HEADS + 1))
            for h in range(HEADS):
                read = split(map_out * table[3 + k][h : h + 1])
                adjoints[h] = adjoints[h] + dot_split(read, bulk[k - 1][cols(h), :])

    for g in range(GROUPS):
        place = ext.at[g]
        place[0:8, :] = tails[me, 16 * g : 16 * g + 16, :].astype(F32)[8:16]
        place[8 : 8 + W, :] = mixer[0, :, cols(g)].astype(F32)
        pre = convolve(place, g)
        sig = sigmoid(pre)
        acts[g] = pre * sig
        slopes[g] = sig + pre * sig * (1.0 - sig)

    map_in, map_out = acts[HEADS], acts[HEADS + 1]
    map_in_s, map_out_s = split(map_in), split(map_out)
    meets = dot_split(map_in_s, map_out_s, NT)
    upper = iota2(0) <= iota2(1)
    lane = iota2(1)
    grad_in = jnp.zeros((W, W), F32)
    grad_out = jnp.zeros((W, W), F32)
    grad_meets = jnp.zeros((W, W), F32)
    sums = jnp.zeros((W, W), F32)
    out_rows, pass_rows, skip_rows = [], [], []

    def with_sum(sums, kind, h, array):
        return jnp.where(lane == HEADS * kind + h, jnp.sum(array, axis=1, keepdims=True), sums)

    for h in range(HEADS):
        cot_b = cotan[0, :, cols(h)]
        cot = cot_b.astype(F32)
        act = acts[h]
        size = column(1, h)
        tail = column(3, h)
        scaled = act * size
        state = states[h]
        adjoint = adjoints[h]
        adjoint_s = split(adjoint)
        falloff = jnp.where(upper, jnp.exp(own_cum[h : h + 1] - column(0, h)), 0.0)
        pair = dot_split(split(scaled), cot_b, NT) * falloff
        grad_meets = grad_meets + pair
        flow = pair * meets
        projected = tail * dot_split(map_in_s, adjoint_s)
        mixed = dot_split(split(falloff * meets), cot_b)
        grad_scaled = mixed + projected
        lead_read = column(2, h) * dot_split(cot_b, split(state), NT)
        grad_out = grad_out + lead_read
        grad_in = grad_in + dot((scaled * tail).astype(BF16), adjoint_s[0], NT)
        out_rows.append(jnp.sum(flow, axis=0, keepdims=True))
        sums = with_sum(sums, 0, h, lead_read * map_out - flow)
        sums = with_sum(sums, 1, h, projected * act)
        sums = with_sum(sums, 2, h, mixed * act)
        passed = jnp.sum(jnp.sum(state * adjoint, axis=0, keepdims=True), axis=1, keepdims=True)
        pass_rows.append(jnp.broadcast_to(passed, (1, W)))
        skip_rows.append(jnp.sum(cot * act, axis=0, keepdims=True))
        grads[h, 0:W, :] = (residual[h] * cot + grad_scaled * size) * slopes[h]
    grad_meets_b = grad_meets.astype(BF16)
    grad_out = grad_out + dot(grad_meets_b, map_in_s[0], TN)
    grad_in = grad_in + dot(grad_meets_b, map_out_s[0])
    grads[HEADS, 0:W, :] = grad_in * slopes[HEADS]
    grads[HEADS + 1, 0:W, :] = grad_out * slopes[HEADS + 1]
    sum_rows = jnp.transpose(sums)

    since = (iota2(0) >= iota2(1)).astype(F32)
    before = (iota2(0) < iota2(1)).astype(F32)
    trail = rows_of(sum_rows, 1)
    grad_decay = (
        dot(jnp.concatenate(out_rows, axis=0) + rows_of(sum_rows, 0), since, precise=True)
        + dot(trail * own_size, before, precise=True)
        + jnp.exp(totals[0]) * jnp.concatenate(pass_rows, axis=0)
    )
    grad_step = grad_decay * rate + rows_of(sum_rows, 2) + trail
    grad_raw = grad_step * sigmoid(rows_of(raw, 0))
    step_grad[0] = grad_raw
    pay[24:28, :] = grad_decay * own_size * rate
    pay[28:32, :] = grad_raw
    pay[32:36, :] = jnp.concatenate(skip_rows, axis=0)
    pay[36:40, :] = jnp.zeros((4, W), F32)

    halo[...] = small_rows([grads[g, 0:8, :][0:3] for g in range(GROUPS)])
    for g in range(GROUPS):
        grads[g, W : W + 8, :] = jnp.zeros((8, W), F32)
        grad = grads[g, 0:W, :]
        for offset in range(TAPS):
            pay[4 * g + offset : 4 * g + offset + 1, :] = jnp.sum(
                grad * ext[g, 5 + offset : 5 + offset + W, :], axis=0, keepdims=True
            )


def rows_body(grads, weight, input_grad, edge):
    for g in range(GROUPS):
        total = grads[g, TAPS - 1 : TAPS - 1 + W, :] * weight[0:1, cols(g)]
        for offset in range(1, TAPS):
            at = TAPS - 1 - offset
            total = total + grads[g, at : at + W, :] * weight[offset : offset + 1, cols(g)]
        input_grad[0, :, cols(g)] = total.astype(BF16)
        edge[:, cols(g)] = total[W - 16 : W]


def merge_body(peers, *refs):
    pay, other, halo = refs[:3]
    parts = refs[3 : 3 + peers]
    total_out, *mixed = refs[3 + peers :]
    total = pay[...] + other[...]
    total_out[...] = total
    pieces = in_pieces(total, MIX_ROWS - SUM_ROW)
    for part, out in zip(parts, mixed):
        out[0:KV_ROWS, :] = part[...]
        out[KV_ROWS:SUM_ROW, :] = halo[...]
        out[SUM_ROW:MIX_ROWS, :] = pieces


def finish_body(peers, count, *refs):
    partial, edge, weight, own, pay = refs[:5]
    mixed = refs[5 : 5 + peers]
    input_grad, key_grad, value_grad, conv_grad, decay_grad, bias_grad, skip_grad = refs[5 + peers :]
    me = lax.axis_index("ctx")
    both = own[...]
    total = pay[...]
    halo = jnp.zeros((32, W), F32)
    for k in range(1, peers + 1):
        other = jnp.bitwise_xor(me, k)
        sent = mixed[k - 1][0:KV_ROWS, :].astype(F32)
        both = both + jnp.where(other > me, sent, 0.0)
        edges = mixed[k - 1][KV_ROWS:SUM_ROW, :].astype(F32)
        halo = halo + jnp.where(other == me + 1, edges, 0.0)
        pieces = mixed[k - 1][SUM_ROW:MIX_ROWS, :].astype(F32)
        total = total + (
            pieces[0:PAY_ROWS] + pieces[PAY_ROWS : 2 * PAY_ROWS] + pieces[2 * PAY_ROWS : 3 * PAY_ROWS]
        )
    key_grad[0] = both[0:W].astype(BF16)
    value_grad[0] = both[W : 2 * W].astype(BF16)
    row = lax.broadcasted_iota(jnp.int32, (16, W), 0)
    for g in range(GROUPS):
        rows = edge[:, cols(g)]
        for offset in range(TAPS - 1):
            for t in range(TAPS - 1 - offset):
                at = 16 - (TAPS - 1 - offset) + t
                piece = halo[3 * g + t : 3 * g + t + 1] * weight[offset : offset + 1, cols(g)]
                rows = rows + jnp.where(row == at, piece, 0.0)
        input_grad[0, 0 : W - 16, cols(g)] = partial[0, 0 : W - 16, cols(g)]
        input_grad[0, W - 16 : W, cols(g)] = rows.astype(BF16)
    total = total * (1.0 / count)
    for g in range(GROUPS):
        conv_grad[:, cols(g)] = total[4 * g : 4 * g + 4]
    sums = jnp.sum(total[24:40], axis=1, keepdims=True)
    for h in range(HEADS):
        decay_grad[h] = jnp.sum(sums[h : h + 1])
        bias_grad[h] = jnp.sum(sums[4 + h : 5 + h])
        skip_grad[h] = jnp.sum(sums[8 + h : 9 + h])


def shape(dims, dtype):
    return jax.ShapeDtypeStruct(dims, dtype)


def on_device(sizes, *args):
    (
        mixer_input,
        step_input,
        conv_weight,
        decay_log,
        step_bias,
        residual,
        mixer_cotangent,
        queries,
        attn_keys,
        attn_values,
        attn_cotangent,
    ) = args
    ctx, dp = sizes["ctx"], sizes["dp"]
    step_input = jnp.swapaxes(step_input, 1, 2)
    peers = ctx - 1
    bits = ctx.bit_length() - 1
    vmem = pl.BlockSpec(memory_space=pltpu.VMEM)
    smem = pl.BlockSpec(memory_space=pltpu.SMEM)

    hbm = pl.BlockSpec(memory_space=pltpu.HBM)
    params = pltpu.CompilerParams(vmem_limit_bytes=LIMIT)
    near, *bulk = pl.pallas_call(
        lambda *refs: pack_body(bits, *refs),
        out_shape=[shape((KV_ROWS, W), BF16)] + [shape((BULK_ROWS, W), BF16)] * bits,
        in_specs=[hbm] * 5,
        out_specs=[vmem] * (1 + bits),
        scratch_shapes=[
            pltpu.VMEM((HEADS, W), F32),
            pltpu.VMEM((16, W), BF16),
            pltpu.VMEM((16, W), BF16),
            pltpu.SemaphoreType.DMA((4 + bits * (GROUPS + 7),)),
        ],
        compiler_params=params,
        name="pack",
    )(
        *(
            pltpu.with_memory_space_constraint(array, pltpu.HBM)
            for array in (mixer_input, step_input, mixer_cotangent, attn_keys, attn_values)
        )
    )

    def swap(array, k, keep=lambda i, j: True, axis="ctx"):
        pairs = [(i, i ^ k) for i in range(sizes[axis]) if keep(i, i ^ k)]
        return lax.ppermute(array, axis, pairs)

    nears = [swap(near, k, lambda i, j: j > i) for k in range(1, ctx)]
    bulks = [swap(bulk[k.bit_length() - 1], k) for k in range(1, ctx)]

    step_grad, grads, halo, pay = pl.pallas_call(
        lambda *refs: mixer_body(peers, *refs),
        out_shape=[
            shape(step_input.shape, F32),
            shape((GROUPS, W + 8, W), F32),
            shape((32, W), BF16),
            shape((PAY_ROWS, W), F32),
        ],
        in_specs=[vmem] * 3 + [smem] * 3 + [vmem] * (1 + peers),
        out_specs=[vmem] * 4,
        scratch_shapes=[
            pltpu.VMEM((ctx + 1, 16 * GROUPS, W), BF16),
            pltpu.VMEM((GROUPS, W + 8, W), F32),
            pltpu.VMEM((peers * GROUPS, W + 8, W), F32),
            pltpu.VMEM((HEADS, W, W), F32),
            pltpu.VMEM((HEADS, W, W), F32),
            pltpu.VMEM((GROUPS, W, W), F32),
            pltpu.VMEM((GROUPS, W, W), F32),
        ],
        compiler_params=params,
        name="mixer",
    )(mixer_input, step_input, conv_weight, decay_log, step_bias, residual, mixer_cotangent, *bulks)

    input_grad, edge = pl.pallas_call(
        rows_body,
        out_shape=[shape(mixer_input.shape, BF16), shape((16, GROUPS * W), F32)],
        in_specs=[vmem] * 2,
        out_specs=[vmem] * 2,
        compiler_params=params,
        name="rows",
    )(grads, conv_weight)

    half, sums = pl.pallas_call(
        lambda *refs: half_body(peers, *refs),
        out_shape=[
            shape((1, W, HEADS // 2 * W), BF16),
            shape((2, ctx * W, W), F32),
        ],
        in_specs=[vmem] * (4 + peers),
        out_specs=[vmem] * 2,
        compiler_params=params,
        name="half",
    )(queries, attn_keys, attn_values, attn_cotangent, *nears)

    query_grad, own, *parts = pl.pallas_call(
        lambda *refs: attend_body(peers, *refs),
        out_shape=[shape(queries.shape, BF16), shape((KV_ROWS, W), F32)]
        + [shape((KV_ROWS, W), BF16)] * peers,
        in_specs=[vmem] * (6 + peers),
        out_specs=[vmem] * (2 + peers),
        compiler_params=params,
        name="attend",
    )(queries, attn_keys, attn_values, attn_cotangent, *nears, half, sums)

    last = dp.bit_length() - 2
    for n in range(last + 1):
        other = swap(pay, 1 << n, axis="dp")
        if n < last:
            pay = pay + other
    pay, *mixed = pl.pallas_call(
        lambda *refs: merge_body(peers, *refs),
        out_shape=[shape((PAY_ROWS, W), F32)] + [shape((MIX_ROWS, W), BF16)] * peers,
        in_specs=[vmem] * (3 + peers),
        out_specs=[vmem] * (1 + peers),
        compiler_params=params,
        name="merge",
    )(pay, other, halo, *parts)
    mixed = [swap(mixed[k - 1], k) for k in range(1, ctx)]
    outs = pl.pallas_call(
        lambda *refs: finish_body(peers, dp, *refs),
        out_shape=[
            shape(mixer_input.shape, BF16),
            shape(attn_keys.shape, BF16),
            shape(attn_values.shape, BF16),
            shape(conv_weight.shape, F32),
        ]
        + [shape((HEADS,), F32)] * 3,
        in_specs=[vmem] * (5 + peers),
        out_specs=[vmem] * 4 + [smem] * 3,
        compiler_params=params,
        name="finish",
    )(input_grad, edge, conv_weight, own, pay, *mixed)
    input_grad, key_grad, value_grad, conv_grad, decay_grad, bias_grad, skip_grad = outs
    return (
        input_grad,
        jnp.swapaxes(step_grad, 1, 2),
        conv_grad,
        decay_grad,
        bias_grad,
        skip_grad,
        query_grad,
        key_grad,
        value_grad,
    )


def solution(mesh):
    split = P("dp", "ctx", None)
    sizes = dict(mesh.shape)

    def step(*args):
        return on_device(sizes, *args)

    return jax.shard_map(
        step,
        mesh=mesh,
        in_specs=(split, split, P(), P(), P(), P(), split, split, split, split, split),
        out_specs=(split, split, P(), P(), P(), P(), split, split, split),
        check_vma=False,
    )
```

```python
import jax
import jax.numpy as jnp
from jax import lax
from jax.experimental import pallas as pl
from jax.experimental.pallas import tpu as pltpu
from jax.sharding import PartitionSpec as P


F32 = jnp.float32
BF16 = jnp.bfloat16
HEADS = 4
TAPS = 4
W = 128
GROUPS = HEADS + 2
KV_ROWS = 2 * W
MIX_ROWS = KV_ROWS + 96
SUM_ROWS = 36
STEP_ROW = (HEADS + 1) * W
BULK_ROWS = STEP_ROW + 16
PAY_ROWS = 40
LIMIT = 16 << 20
LOG2E = 1.4426950408889634


def dot(a, b, dims=((1,), (0,)), precise=False):
    return lax.dot_general(
        a,
        b,
        (dims, ((), ())),
        precision=lax.Precision.HIGHEST if precise else None,
        preferred_element_type=F32,
    )


def split(array):
    high = array.astype(BF16)
    return high, (array - high.astype(F32)).astype(BF16)


def dot_split(a, b, dims=((1,), (0,))):
    a = a if isinstance(a, tuple) else (a,)
    b = b if isinstance(b, tuple) else (b,)
    total = dot(a[0], b[0], dims)
    if len(a) > 1:
        total = total + dot(a[1], b[0], dims)
    if len(b) > 1:
        total = total + dot(a[0], b[1], dims)
    return total


NT = ((1,), (1,))
TN = ((0,), (0,))


def iota2(dim):
    return lax.broadcasted_iota(jnp.int32, (W, W), dim)


def cols(g):
    return slice(g * W, (g + 1) * W)


def in_pieces(rows, count):
    high = rows.astype(BF16).astype(F32)
    mid = (rows - high).astype(BF16).astype(F32)
    low = rows - high - mid
    parts = [high, mid, low]
    if count > 3 * rows.shape[0]:
        parts.append(jnp.zeros((count - 3 * rows.shape[0], W), F32))
    return jnp.concatenate(parts, axis=0).astype(BF16)


def pack_body(bits, mixer, step, cotan, keys, values, decay_log, bias, residual, near, *refs):
    bulk, (consts, size, ends, extra, scalars, sems) = refs[:bits], refs[bits:]
    me = lax.axis_index("ctx")

    def copy(source, target, at):
        return pltpu.make_async_copy(source, target, sems.at[at])

    first = [
        copy(step.at[0], size, 0),
        copy(keys.at[0], near.at[0:W, :], 1),
        copy(values.at[0], near.at[W : 2 * W, :], 2),
        copy(mixer.at[0, W - 16 : W, cols(HEADS + 1)], ends, 3),
    ] + [
        copy(source, scalars.at[n], 4 + n) for n, source in enumerate((decay_log, bias, residual))
    ]
    for c in first:
        c.start()
    later = [jnp.bitwise_and(lax.shift_right_logical(me, b), 1) == 0 for b in range(bits)]
    forward, backward = [], []
    for b in range(bits):
        at = 7 + b * (GROUPS + 6)
        forward.append(
            [
                copy(mixer.at[0, :, cols(g)], bulk[b].at[cols(g), :], at + g)
                for g in range(HEADS + 1)
            ]
        )
        backward.append(
            [
                copy(cotan.at[0, :, cols(g)], bulk[b].at[cols(g), :], at + GROUPS + g)
                for g in range(HEADS)
            ]
            + [
                copy(
                    mixer.at[0, :, cols(HEADS + 1)],
                    bulk[b].at[cols(HEADS), :],
                    at + GROUPS + HEADS,
                )
            ]
        )

        @pl.when(later[b])
        def _(b=b):
            for c in forward[b]:
                c.start()

        @pl.when(jnp.logical_not(later[b]))
        def _(b=b):
            for c in backward[b]:
                c.start()

    for c in first:
        c.wait()
    rows = [jnp.full((1, W), scalars[n, h], F32) for n in range(3) for h in range(HEADS)]
    rate = -jnp.exp(jnp.concatenate(rows[:HEADS], axis=0))
    consts[...] = jnp.concatenate([rate] + rows[HEADS:] + [jnp.zeros((HEADS, W), F32)], axis=0)
    pieces = in_pieces(size[...], 12).astype(F32)
    last = ends[...].astype(F32)[12:16]
    extra[...] = jnp.concatenate([pieces, last], axis=0).astype(BF16)
    for b in range(bits):
        at = 7 + bits * (GROUPS + 6) + b
        sized = copy(extra, bulk[b].at[STEP_ROW:BULK_ROWS, :], at)
        forward[b].append(sized)
        backward[b].append(sized)
        sized.start()

        @pl.when(later[b])
        def _(b=b):
            for c in forward[b]:
                c.wait()

        @pl.when(jnp.logical_not(later[b]))
        def _(b=b):
            for c in backward[b]:
                c.wait()


def attend_heads(peers, heads, queries, keys, values, cotan, near, query_grad, sums):
    me = lax.axis_index("ctx")
    scale = W ** (-0.5)
    keys_all = jnp.concatenate([keys[0]] + [m[0:W, :] for m in near], axis=0)
    values_all = jnp.concatenate([values[0]] + [m[W : 2 * W, :] for m in near], axis=0)
    causal = iota2(0) >= iota2(1)
    rounded_heads, dscore_heads = [], []
    for r in heads:
        query = queries[0, :, cols(r)]
        cot = cotan[0, :, cols(r)]
        scores = dot(query, keys_all, NT) * (scale * LOG2E)
        blocks = [jnp.where(causal, scores[:, 0:W], -jnp.inf)]
        for k in range(1, peers + 1):
            bit = k.bit_length() - 1
            earlier = jnp.bitwise_and(lax.shift_right_logical(me, bit), 1) == 1
            blocks.append(jnp.where(earlier, scores[:, cols(k)], -jnp.inf))
        scores = jnp.concatenate(blocks, axis=1)
        top = jnp.max(scores, axis=1, keepdims=True)
        weights = jnp.exp2(scores - top)
        probs = weights * (1.0 / jnp.sum(weights, axis=1, keepdims=True))
        rounded = probs.astype(BF16)
        attended = dot(rounded, values_all)
        delta = jnp.sum(cot.astype(F32) * attended, axis=1, keepdims=True)
        dprob = dot(cot, values_all, NT)
        dscore = (probs * (dprob - delta) * scale).astype(BF16)
        query_grad[0, :, cols(r)] = dot(dscore, keys_all).astype(BF16)
        rounded_heads.append(rounded)
        dscore_heads.append(dscore)
    query_rows = jnp.concatenate([queries[0, :, cols(r)] for r in heads], axis=0)
    cotan_rows = jnp.concatenate([cotan[0, :, cols(r)] for r in heads], axis=0)
    key_acc = dot(jnp.concatenate(dscore_heads, axis=0), query_rows, TN)
    value_acc = dot(jnp.concatenate(rounded_heads, axis=0), cotan_rows, TN)
    if sums is not None:
        key_acc, value_acc = key_acc + sums[0], value_acc + sums[1]
    return key_acc, value_acc


def half_body(peers, *refs):
    near = refs[4 : 4 + peers]
    query_grad, sums = refs[4 + peers :]
    sums[0], sums[1] = attend_heads(peers, range(HEADS // 2), *refs[:4], near, query_grad, None)


def attend_body(peers, *refs):
    near = refs[4 : 4 + peers]
    half, sums, query_grad, own, *parts = refs[4 + peers :]
    query_grad[0, :, 0 : HEADS // 2 * W] = half[0]
    key_acc, value_acc = attend_heads(
        peers, range(HEADS // 2, HEADS), *refs[:4], near, query_grad, sums
    )
    own[0:W, :] = key_acc[0:W]
    own[W : 2 * W, :] = value_acc[0:W]
    for k in range(1, peers + 1):
        parts[k - 1][0:W, :] = key_acc[cols(k)].astype(BF16)
        parts[k - 1][W : 2 * W, :] = value_acc[cols(k)].astype(BF16)


def sigmoid(v):
    return 0.5 * jnp.tanh(0.5 * v) + 0.5


def convolve(weight, place, g, count=W):
    total = place[5 : 5 + count, :] * weight[0:1, cols(g)]
    for offset in range(1, TAPS):
        at = 5 + offset
        total = total + place[at : at + count, :] * weight[offset : offset + 1, cols(g)]
    return total


def step_table(pieces, bias, rate):
    slots = len(pieces)
    raw = jnp.concatenate(pieces, axis=0) + jnp.concatenate([bias] * slots, axis=0)
    sizes = jnp.maximum(raw, 0.0) + jnp.log(1.0 + jnp.exp(-jnp.abs(raw)))
    decays = sizes * jnp.concatenate([rate] * slots, axis=0)
    upto = (iota2(0) <= iota2(1)).astype(F32)
    return raw, sizes, dot(decays, upto, precise=True)


def as_columns(table):
    used = HEADS * len(table)
    columns = jnp.transpose(jnp.concatenate(table + [jnp.zeros((W - used, W), F32)], axis=0))

    def column(group, h):
        at = HEADS * group + h
        return columns[:, at : at + 1]

    return column


def with_sum(sums, kind, h, array):
    lane = lax.broadcasted_iota(jnp.int32, sums.shape, 1)
    return jnp.where(lane == HEADS * kind + h, jnp.sum(array, axis=1, keepdims=True), sums)


def join(top, rest):
    return jnp.concatenate([top, rest], axis=0)


def own_body(mixer, step, weight, consts, cotan, *outs):
    ext, acts, slopes, mixed_out, maps, sums_out, rows_out = outs
    first = iota2(0) < TAPS - 1
    for g in range(GROUPS):
        place = ext.at[g]
        place[0:8, :] = jnp.zeros((8, W), F32)
        place[8 : 8 + W, :] = mixer[0, :, cols(g)].astype(F32)
        pre = convolve(weight, place, g)
        sig = sigmoid(pre)
        acts[g] = jnp.where(first, 0.0, pre * sig)
        slopes[g] = sig + pre * sig * (1.0 - sig)
    _, size, cum = step_table([step[0]], consts[4:8], consts[0:4])
    column = as_columns([cum, size])
    map_in_s, map_out_s = split(acts[HEADS]), split(acts[HEADS + 1])
    meets = dot_split(map_in_s, map_out_s, NT)
    upper = iota2(0) <= iota2(1)
    grad_meets = jnp.zeros((W, W), F32)
    sums = jnp.zeros((W, W), F32)
    out_rows, skip_rows = [], []
    for h in range(HEADS):
        cot_b = cotan[0, :, cols(h)]
        act = acts[h]
        falloff = jnp.where(upper, jnp.exp(cum[h : h + 1] - column(0, h)), 0.0)
        pair = dot_split(split(act * column(1, h)), cot_b, NT) * falloff
        grad_meets = grad_meets + pair
        flow = pair * meets
        mixed = dot_split(split(falloff * meets), cot_b)
        mixed_out[h] = mixed
        out_rows.append(jnp.sum(flow, axis=0, keepdims=True))
        sums = with_sum(sums, 0, h, -flow)
        sums = with_sum(sums, 2, h, mixed * act)
        skip_rows.append(jnp.sum(cot_b.astype(F32) * act, axis=0, keepdims=True))
    grad_meets_b = grad_meets.astype(BF16)
    maps[0] = dot(grad_meets_b, map_out_s[0])
    maps[1] = dot(grad_meets_b, map_in_s[0], TN)
    sums_out[...] = sums
    rows_out[...] = jnp.concatenate(out_rows + skip_rows, axis=0)


def mixer_body(peers, *refs):
    mixer, step, weight, consts, cotan = refs[:5]
    ext, acts, slopes, mixed_in, maps, sums_in, rows_in = refs[5:12]
    bulk = refs[12 : 12 + peers]
    grads, halo, pay = refs[12 + peers : 15 + peers]
    tails, first_ext, peer_ext, states, adjoints = refs[15 + peers :]
    me = lax.axis_index("ctx")
    slots = peers + 1
    index = [me] + [jnp.bitwise_xor(me, k) for k in range(1, slots)]

    tails[0] = jnp.zeros((16 * GROUPS, W), BF16)
    for g in range(GROUPS):
        tails[me + 1, 16 * g : 16 * g + 16, :] = mixer[0, W - 16 : W, cols(g)]
    for k in range(1, slots):
        earlier = index[k] < me

        @pl.when(earlier)
        def _(k=k):
            for g in range(HEADS + 1):
                tails[index[k] + 1, 16 * g : 16 * g + 16, :] = bulk[k - 1][
                    (g + 1) * W - 16 : (g + 1) * W, :
                ]
            tails[index[k] + 1, 16 * (GROUPS - 1) : 16 * GROUPS, :] = bulk[k - 1][
                STEP_ROW:BULK_ROWS, :
            ]

        @pl.when(jnp.logical_not(earlier))
        def _(k=k):
            tails[index[k] + 1, 16 * (GROUPS - 1) : 16 * GROUPS, :] = bulk[k - 1][
                STEP_ROW - 16 : STEP_ROW, :
            ]

    pieces = [step[0]]
    for k in range(1, slots):
        sent = bulk[k - 1][STEP_ROW:BULK_ROWS, :].astype(F32)
        pieces.append(sent[0:4] + sent[4:8] + sent[8:12])
    rate, bias = consts[0:4], consts[4:8]
    raw, sizes, cumulative = step_table(pieces, bias, rate)

    def rows_of(array, k):
        return array[HEADS * k : HEADS * (k + 1)]

    totals = [
        jnp.broadcast_to(rows_of(cumulative, k)[:, W - 1 : W], (HEADS, W)) for k in range(slots)
    ]
    own_cum = rows_of(cumulative, 0)
    own_size = rows_of(sizes, 0)
    table = [own_cum, own_size, jnp.exp(own_cum), jnp.exp(totals[0] - own_cum)]
    for k in range(1, slots):
        low, high = jnp.minimum(me, index[k]), jnp.maximum(me, index[k])
        between = jnp.zeros((HEADS, W), F32)
        for m in range(1, slots):
            inside = jnp.logical_and(index[m] > low, index[m] < high)
            between = between + jnp.where(inside, totals[m], 0.0)
        earlier = index[k] < me
        cum = rows_of(cumulative, k)
        span = jnp.where(earlier, totals[k] - cum, cum) + between
        table.append(jnp.exp(span) * jnp.where(earlier, rows_of(sizes, k), 1.0))
    column = as_columns(table)

    def peer_act(k, at, g):
        place = peer_ext.at[(k - 1) * GROUPS + g]
        place[0:8, :] = tails[index[k], 16 * g : 16 * g + 16, :].astype(F32)[8:16]
        place[8 : 8 + W, :] = bulk[k - 1][cols(at), :].astype(F32)
        pre = convolve(weight, place, g)
        return pre * sigmoid(pre)

    states[...] = jnp.zeros_like(states)
    adjoints[...] = jnp.zeros_like(adjoints)
    for k in range(1, slots):
        earlier = index[k] < me

        @pl.when(earlier)
        def _(k=k):
            map_in = split(jnp.transpose(peer_act(k, HEADS, HEADS)))
            for h in range(HEADS):
                rows = split(peer_act(k, h, h) * column(3 + k, h))
                states[h] = states[h] + dot_split(map_in, rows)

        @pl.when(jnp.logical_not(earlier))
        def _(k=k):
            map_out = jnp.transpose(peer_act(k, HEADS, HEADS + 1))
            for h in range(HEADS):
                read = split(map_out * table[3 + k][h : h + 1])
                adjoints[h] = adjoints[h] + dot_split(read, bulk[k - 1][cols(h), :])

    early = lax.broadcasted_iota(jnp.int32, (8, W), 0) < TAPS - 1
    first_acts, first_slopes, new_acts = [], [], []
    for g in range(GROUPS):
        place = first_ext.at[g]
        place[0:8, :] = tails[me, 16 * g : 16 * g + 16, :].astype(F32)[8:16]
        place[8:16, :] = ext[g, 8:16, :]
        pre = convolve(weight, place, g, 8)
        sig = sigmoid(pre)
        first_acts.append(pre * sig)
        first_slopes.append(sig + pre * sig * (1.0 - sig))
        new_acts.append(jnp.where(early, pre * sig, 0.0))

    def act_of(g):
        return join(first_acts[g], acts[g, 8:W, :])

    def slope_of(g):
        return join(first_slopes[g], slopes[g, 8:W, :])

    map_in, map_out = act_of(HEADS), act_of(HEADS + 1)
    map_in_s, map_out_s = split(map_in), split(map_out)
    new_in = new_acts[HEADS]
    new_meets = dot_split(split(new_in), map_out_s, NT)
    upper = lax.broadcasted_iota(jnp.int32, (8, W), 0) <= lax.broadcasted_iota(
        jnp.int32, (8, W), 1
    )
    grad_in, grad_out = maps[0], maps[1]
    new_grad_meets = jnp.zeros((8, W), F32)
    sums = sums_in[...]
    out_rows, pass_rows, skip_rows = [], [], []

    for h in range(HEADS):
        cot_b = cotan[0, :, cols(h)]
        cot = cot_b.astype(F32)
        act = act_of(h)
        new_act = new_acts[h]
        size = column(1, h)
        tail = column(3, h)
        state = states[h]
        adjoint = adjoints[h]
        adjoint_s = split(adjoint)
        falloff = jnp.where(upper, jnp.exp(own_cum[h : h + 1] - column(0, h)[0:8]), 0.0)
        pair = dot_split(split(new_act * size[0:8]), cot_b, NT) * falloff
        new_grad_meets = new_grad_meets + pair
        flow = pair * new_meets
        new_mixed = dot_split(split(falloff * new_meets), cot_b)
        projected = tail * dot_split(map_in_s, adjoint_s)
        mixed = mixed_in[h]
        mixed = join(mixed[0:8] + new_mixed, mixed[8:W])
        grad_scaled = mixed + projected
        lead_read = column(2, h) * dot_split(cot_b, split(state), NT)
        grad_out = grad_out + lead_read
        grad_in = grad_in + dot((act * size * tail).astype(BF16), adjoint_s[0], NT)
        out_rows.append(rows_in[h : h + 1] + jnp.sum(flow, axis=0, keepdims=True))
        carried = lead_read * map_out
        trailing = projected * act
        carried = join(carried[0:8] - flow, carried[8:W])
        extra = with_sum(jnp.zeros((W, W), F32), 0, h, carried)
        extra = with_sum(extra, 1, h, trailing)
        extra8 = with_sum(jnp.zeros((8, W), F32), 2, h, new_mixed * new_act)
        sums = sums + extra
        sums = join(sums[0:8] + extra8, sums[8:W])
        passed = jnp.sum(jnp.sum(state * adjoint, axis=0, keepdims=True), axis=1, keepdims=True)
        pass_rows.append(jnp.broadcast_to(passed, (1, W)))
        skipped = jnp.sum(cot[0:8] * new_act, axis=0, keepdims=True)
        skip_rows.append(rows_in[HEADS + h : HEADS + h + 1] + skipped)
        grads[h, 0:W, :] = (consts[8 + h : 9 + h] * cot + grad_scaled * size) * slope_of(h)
    new_b = new_grad_meets.astype(BF16)
    grad_out = grad_out + dot(new_b, new_in.astype(BF16), TN)
    grad_in = join(grad_in[0:8] + dot(new_b, map_out_s[0]), grad_in[8:W])
    grads[HEADS, 0:W, :] = grad_in * slope_of(HEADS)
    grads[HEADS + 1, 0:W, :] = grad_out * slope_of(HEADS + 1)
    sum_rows = jnp.transpose(sums)

    since = (iota2(0) >= iota2(1)).astype(F32)
    before = (iota2(0) < iota2(1)).astype(F32)
    trail = rows_of(sum_rows, 1)
    grad_decay = (
        dot(jnp.concatenate(out_rows, axis=0) + rows_of(sum_rows, 0), since, precise=True)
        + dot(trail * own_size, before, precise=True)
        + jnp.exp(totals[0]) * jnp.concatenate(pass_rows, axis=0)
    )
    grad_step = grad_decay * rate + rows_of(sum_rows, 2) + trail
    grad_raw = grad_step * sigmoid(rows_of(raw, 0))
    pay[24:28, :] = grad_decay * own_size * rate
    pay[28:32, :] = grad_raw
    pay[32:36, :] = jnp.concatenate(skip_rows, axis=0)
    pay[36:40, :] = jnp.zeros((4, W), F32)

    for g in range(GROUPS):
        halo[8 * g : 8 * g + 8, :] = grads[g, 0:8, :]
    for g in range(GROUPS):
        grads[g, W : W + 8, :] = jnp.zeros((8, W), F32)
        grad = grads[g, 0:W, :]
        for offset in range(TAPS):
            pay[4 * g + offset : 4 * g + offset + 1, :] = jnp.sum(
                grad * join(
                    first_ext[g, 5 + offset : 13 + offset, :],
                    ext[g, 13 + offset : 5 + offset + W, :],
                ),
                axis=0,
                keepdims=True,
            )


def rows_body(grads, weight, pay, input_grad, edge, step_grad):
    step_grad[0] = pay[28:32, :]
    for g in range(GROUPS):
        total = grads[g, TAPS - 1 : TAPS - 1 + W, :] * weight[0:1, cols(g)]
        for offset in range(1, TAPS):
            at = TAPS - 1 - offset
            total = total + grads[g, at : at + W, :] * weight[offset : offset + 1, cols(g)]
        input_grad[0, :, cols(g)] = total.astype(BF16)
        edge[:, cols(g)] = total[W - 16 : W]


def merge_body(peers, *refs):
    pay, other, halo = refs[:3]
    parts = refs[3 : 3 + peers]
    total_out, *mixed = refs[3 + peers :]
    total = pay[...] + other[...]
    total_out[...] = total
    sums = total[0:SUM_ROWS]
    high = sums.astype(BF16).astype(F32)
    edges = [halo[8 * g : 8 * g + 3, :] for g in range(GROUPS)]
    rest = jnp.zeros((MIX_ROWS - KV_ROWS - 2 * SUM_ROWS - 3 * GROUPS, W), F32)
    pieces = jnp.concatenate([high, sums - high] + edges + [rest], axis=0).astype(BF16)
    for part, out in zip(parts, mixed):
        out[0:KV_ROWS, :] = part[...]
        out[KV_ROWS:MIX_ROWS, :] = pieces


def finish_body(peers, count, *refs):
    partial, edge, weight, own, pay = refs[:5]
    mixed = refs[5 : 5 + peers]
    input_grad, key_grad, value_grad, conv_grad, decay_grad, bias_grad, skip_grad = refs[5 + peers :]
    me = lax.axis_index("ctx")
    both = own[...]
    total = pay[0:SUM_ROWS, :]
    halo = jnp.zeros((3 * GROUPS, W), F32)
    for k in range(1, peers + 1):
        other = jnp.bitwise_xor(me, k)
        sent = mixed[k - 1][0:KV_ROWS, :].astype(F32)
        both = both + jnp.where(other > me, sent, 0.0)
        pieces = mixed[k - 1][KV_ROWS:MIX_ROWS, :].astype(F32)
        total = total + pieces[0:SUM_ROWS] + pieces[SUM_ROWS : 2 * SUM_ROWS]
        edges = pieces[2 * SUM_ROWS : 2 * SUM_ROWS + 3 * GROUPS]
        halo = halo + jnp.where(other == me + 1, edges, 0.0)
    key_grad[0] = both[0:W].astype(BF16)
    value_grad[0] = both[W : 2 * W].astype(BF16)
    row = lax.broadcasted_iota(jnp.int32, (16, W), 0)
    for g in range(GROUPS):
        rows = edge[:, cols(g)]
        for offset in range(TAPS - 1):
            for t in range(TAPS - 1 - offset):
                at = 16 - (TAPS - 1 - offset) + t
                piece = halo[3 * g + t : 3 * g + t + 1] * weight[offset : offset + 1, cols(g)]
                rows = rows + jnp.where(row == at, piece, 0.0)
        input_grad[0, 0 : W - 16, cols(g)] = partial[0, 0 : W - 16, cols(g)]
        input_grad[0, W - 16 : W, cols(g)] = rows.astype(BF16)
    total = total * (1.0 / count)
    for g in range(GROUPS):
        conv_grad[:, cols(g)] = total[4 * g : 4 * g + 4]
    sums = jnp.sum(total[24:SUM_ROWS], axis=1, keepdims=True)
    for h in range(HEADS):
        decay_grad[h] = jnp.sum(sums[h : h + 1])
        bias_grad[h] = jnp.sum(sums[4 + h : 5 + h])
        skip_grad[h] = jnp.sum(sums[8 + h : 9 + h])


def shape(dims, dtype):
    return jax.ShapeDtypeStruct(dims, dtype)


def on_device(sizes, *args):
    (
        mixer_input,
        step_input,
        conv_weight,
        decay_log,
        step_bias,
        residual,
        mixer_cotangent,
        queries,
        attn_keys,
        attn_values,
        attn_cotangent,
    ) = args
    ctx, dp = sizes["ctx"], sizes["dp"]
    step_input = jnp.swapaxes(step_input, 1, 2)
    peers = ctx - 1
    bits = ctx.bit_length() - 1
    vmem = pl.BlockSpec(memory_space=pltpu.VMEM)
    smem = pl.BlockSpec(memory_space=pltpu.SMEM)

    hbm = pl.BlockSpec(memory_space=pltpu.HBM)
    params = pltpu.CompilerParams(vmem_limit_bytes=LIMIT)
    near, *bulk, consts = pl.pallas_call(
        lambda *refs: pack_body(bits, *refs),
        out_shape=[shape((KV_ROWS, W), BF16)] + [shape((BULK_ROWS, W), BF16)] * bits
        + [shape((4 * HEADS, W), F32)],
        in_specs=[hbm] * 8,
        out_specs=[vmem] * (2 + bits),
        scratch_shapes=[
            pltpu.VMEM((HEADS, W), F32),
            pltpu.VMEM((16, W), BF16),
            pltpu.VMEM((16, W), BF16),
            pltpu.SMEM((3, HEADS), F32),
            pltpu.SemaphoreType.DMA((7 + bits * (GROUPS + 7),)),
        ],
        compiler_params=params,
        name="pack",
    )(
        *(
            pltpu.with_memory_space_constraint(array, pltpu.HBM)
            for array in (
                mixer_input,
                step_input,
                mixer_cotangent,
                attn_keys,
                attn_values,
                decay_log,
                step_bias,
                residual,
            )
        )
    )

    def swap(array, k, keep=lambda i, j: True, axis="ctx"):
        pairs = [(i, i ^ k) for i in range(sizes[axis]) if keep(i, i ^ k)]
        return lax.ppermute(array, axis, pairs)

    nears = [swap(near, k, lambda i, j: j > i) for k in range(1, ctx)]
    bulks = [swap(bulk[k.bit_length() - 1], k) for k in range(1, ctx)]

    kept = pl.pallas_call(
        own_body,
        out_shape=[
            shape((GROUPS, W + 8, W), F32),
            shape((GROUPS, W, W), F32),
            shape((GROUPS, W, W), F32),
            shape((HEADS, W, W), F32),
            shape((2, W, W), F32),
            shape((W, W), F32),
            shape((2 * HEADS, W), F32),
        ],
        in_specs=[vmem] * 5,
        out_specs=[vmem] * 7,
        compiler_params=params,
        name="own",
    )(
        mixer_input,
        step_input,
        conv_weight,
        consts,
        mixer_cotangent,
    )

    grads, halo, pay = pl.pallas_call(
        lambda *refs: mixer_body(peers, *refs),
        out_shape=[
            shape((GROUPS, W + 8, W), F32),
            shape((8 * GROUPS, W), F32),
            shape((PAY_ROWS, W), F32),
        ],
        in_specs=[vmem] * (12 + peers),
        out_specs=[vmem] * 3,
        scratch_shapes=[
            pltpu.VMEM((ctx + 1, 16 * GROUPS, W), BF16),
            pltpu.VMEM((GROUPS, 24, W), F32),
            pltpu.VMEM((peers * GROUPS, W + 8, W), F32),
            pltpu.VMEM((HEADS, W, W), F32),
            pltpu.VMEM((HEADS, W, W), F32),
        ],
        compiler_params=params,
        name="mixer",
    )(
        mixer_input,
        step_input,
        conv_weight,
        consts,
        mixer_cotangent,
        *kept,
        *bulks,
    )

    input_grad, edge, step_grad = pl.pallas_call(
        rows_body,
        out_shape=[
            shape(mixer_input.shape, BF16),
            shape((16, GROUPS * W), F32),
            shape(step_input.shape, F32),
        ],
        in_specs=[vmem] * 3,
        out_specs=[vmem] * 3,
        compiler_params=params,
        name="rows",
    )(grads, conv_weight, pay)

    half, sums = pl.pallas_call(
        lambda *refs: half_body(peers, *refs),
        out_shape=[
            shape((1, W, HEADS // 2 * W), BF16),
            shape((2, ctx * W, W), F32),
        ],
        in_specs=[vmem] * (4 + peers),
        out_specs=[vmem] * 2,
        compiler_params=params,
        name="half",
    )(queries, attn_keys, attn_values, attn_cotangent, *nears)

    query_grad, own, *parts = pl.pallas_call(
        lambda *refs: attend_body(peers, *refs),
        out_shape=[shape(queries.shape, BF16), shape((KV_ROWS, W), F32)]
        + [shape((KV_ROWS, W), BF16)] * peers,
        in_specs=[vmem] * (6 + peers),
        out_specs=[vmem] * (2 + peers),
        compiler_params=params,
        name="attend",
    )(queries, attn_keys, attn_values, attn_cotangent, *nears, half, sums)

    last = dp.bit_length() - 2
    for n in range(last + 1):
        other = swap(pay, 1 << n, axis="dp")
        if n < last:
            pay = pay + other
    pay, *mixed = pl.pallas_call(
        lambda *refs: merge_body(peers, *refs),
        out_shape=[shape((PAY_ROWS, W), F32)] + [shape((MIX_ROWS, W), BF16)] * peers,
        in_specs=[vmem] * (3 + peers),
        out_specs=[vmem] * (1 + peers),
        compiler_params=params,
        name="merge",
    )(pay, other, halo, *parts)
    mixed = [swap(mixed[k - 1], k) for k in range(1, ctx)]
    outs = pl.pallas_call(
        lambda *refs: finish_body(peers, dp, *refs),
        out_shape=[
            shape(mixer_input.shape, BF16),
            shape(attn_keys.shape, BF16),
            shape(attn_values.shape, BF16),
            shape(conv_weight.shape, F32),
        ]
        + [shape((HEADS,), F32)] * 3,
        in_specs=[vmem] * (5 + peers),
        out_specs=[vmem] * 4 + [smem] * 3,
        compiler_params=params,
        name="finish",
    )(input_grad, edge, conv_weight, own, pay, *mixed)
    input_grad, key_grad, value_grad, conv_grad, decay_grad, bias_grad, skip_grad = outs
    return (
        input_grad,
        jnp.swapaxes(step_grad, 1, 2),
        conv_grad,
        decay_grad,
        bias_grad,
        skip_grad,
        query_grad,
        key_grad,
        value_grad,
    )


def solution(mesh):
    split = P("dp", "ctx", None)
    sizes = dict(mesh.shape)

    def step(*args):
        return on_device(sizes, *args)

    return jax.shard_map(
        step,
        mesh=mesh,
        in_specs=(split, split, P(), P(), P(), P(), split, split, split, split, split),
        out_specs=(split, split, P(), P(), P(), P(), split, split, split),
        check_vma=False,
    )
```

```python
import jax
import jax.numpy as jnp
from jax import lax
from jax.experimental import pallas as pl
from jax.experimental.pallas import tpu as pltpu
from jax.sharding import PartitionSpec as P


F32 = jnp.float32
BF16 = jnp.bfloat16
HEADS = 4
TAPS = 4
W = 128
GROUPS = HEADS + 2
KV_ROWS = 2 * W
MIX_ROWS = KV_ROWS + 96
SUM_ROWS = 36
STEP_ROW = (HEADS + 1) * W
BULK_ROWS = STEP_ROW + 16
PAY_ROWS = 40
LIMIT = 16 << 20
LOG2E = 1.4426950408889634


def dot(a, b, dims=((1,), (0,)), precise=False):
    return lax.dot_general(
        a,
        b,
        (dims, ((), ())),
        precision=lax.Precision.HIGHEST if precise else None,
        preferred_element_type=F32,
    )


def split(array):
    high = array.astype(BF16)
    return high, (array - high.astype(F32)).astype(BF16)


def dot_split(a, b, dims=((1,), (0,))):
    a = a if isinstance(a, tuple) else (a,)
    b = b if isinstance(b, tuple) else (b,)
    total = dot(a[0], b[0], dims)
    if len(a) > 1:
        total = total + dot(a[1], b[0], dims)
    if len(b) > 1:
        total = total + dot(a[0], b[1], dims)
    return total


NT = ((1,), (1,))
TN = ((0,), (0,))


def iota2(dim):
    return lax.broadcasted_iota(jnp.int32, (W, W), dim)


def cols(g):
    return slice(g * W, (g + 1) * W)


def in_pieces(rows, count):
    high = rows.astype(BF16).astype(F32)
    mid = (rows - high).astype(BF16).astype(F32)
    low = rows - high - mid
    parts = [high, mid, low]
    if count > 3 * rows.shape[0]:
        parts.append(jnp.zeros((count - 3 * rows.shape[0], W), F32))
    return jnp.concatenate(parts, axis=0).astype(BF16)


def pack_body(bits, mixer, step, cotan, keys, values, decay_log, bias, residual, near, *refs):
    bulk, (consts, size, ends, extra, scalars, sems) = refs[:bits], refs[bits:]
    me = lax.axis_index("ctx")

    def copy(source, target, at):
        return pltpu.make_async_copy(source, target, sems.at[at])

    first = [
        copy(step.at[0], size, 0),
        copy(keys.at[0], near.at[0:W, :], 1),
        copy(values.at[0], near.at[W : 2 * W, :], 2),
        copy(mixer.at[0, W - 16 : W, cols(HEADS + 1)], ends, 3),
    ] + [
        copy(source, scalars.at[n], 4 + n) for n, source in enumerate((decay_log, bias, residual))
    ]
    for c in first:
        c.start()
    later = [jnp.bitwise_and(lax.shift_right_logical(me, b), 1) == 0 for b in range(bits)]
    forward, backward = [], []
    for b in range(bits):
        at = 7 + b * (GROUPS + 6)
        forward.append(
            [
                copy(mixer.at[0, :, cols(g)], bulk[b].at[cols(g), :], at + g)
                for g in range(HEADS + 1)
            ]
        )
        backward.append(
            [
                copy(cotan.at[0, :, cols(g)], bulk[b].at[cols(g), :], at + GROUPS + g)
                for g in range(HEADS)
            ]
            + [
                copy(
                    mixer.at[0, :, cols(HEADS + 1)],
                    bulk[b].at[cols(HEADS), :],
                    at + GROUPS + HEADS,
                )
            ]
        )

        @pl.when(later[b])
        def _(b=b):
            for c in forward[b]:
                c.start()

        @pl.when(jnp.logical_not(later[b]))
        def _(b=b):
            for c in backward[b]:
                c.start()

    for c in first:
        c.wait()
    rows = [jnp.full((1, W), scalars[n, h], F32) for n in range(3) for h in range(HEADS)]
    rate = -jnp.exp(jnp.concatenate(rows[:HEADS], axis=0))
    consts[...] = jnp.concatenate([rate] + rows[HEADS:] + [jnp.zeros((HEADS, W), F32)], axis=0)
    pieces = in_pieces(size[...], 12).astype(F32)
    last = ends[...].astype(F32)[12:16]
    extra[...] = jnp.concatenate([pieces, last], axis=0).astype(BF16)
    for b in range(bits):
        at = 7 + bits * (GROUPS + 6) + b
        sized = copy(extra, bulk[b].at[STEP_ROW:BULK_ROWS, :], at)
        forward[b].append(sized)
        backward[b].append(sized)
        sized.start()

        @pl.when(later[b])
        def _(b=b):
            for c in forward[b]:
                c.wait()

        @pl.when(jnp.logical_not(later[b]))
        def _(b=b):
            for c in backward[b]:
                c.wait()


def attend_heads(peers, heads, queries, keys, values, cotan, near, query_grad, sums):
    me = lax.axis_index("ctx")
    scale = W ** (-0.5)
    keys_all = jnp.concatenate([keys[0]] + [m[0:W, :] for m in near], axis=0)
    values_all = jnp.concatenate([values[0]] + [m[W : 2 * W, :] for m in near], axis=0)
    causal = iota2(0) >= iota2(1)
    rounded_heads, dscore_heads = [], []
    for r in heads:
        query = queries[0, :, cols(r)]
        cot = cotan[0, :, cols(r)]
        scores = dot(query, keys_all, NT) * (scale * LOG2E)
        blocks = [jnp.where(causal, scores[:, 0:W], -jnp.inf)]
        for k in range(1, peers + 1):
            bit = k.bit_length() - 1
            earlier = jnp.bitwise_and(lax.shift_right_logical(me, bit), 1) == 1
            blocks.append(jnp.where(earlier, scores[:, cols(k)], -jnp.inf))
        scores = jnp.concatenate(blocks, axis=1)
        top = jnp.max(scores, axis=1, keepdims=True)
        weights = jnp.exp2(scores - top)
        probs = weights * (1.0 / jnp.sum(weights, axis=1, keepdims=True))
        rounded = probs.astype(BF16)
        attended = dot(rounded, values_all)
        delta = jnp.sum(cot.astype(F32) * attended, axis=1, keepdims=True)
        dprob = dot(cot, values_all, NT)
        dscore = (probs * (dprob - delta) * scale).astype(BF16)
        query_grad[0, :, cols(r - heads[0])] = dot(dscore, keys_all).astype(BF16)
        rounded_heads.append(rounded)
        dscore_heads.append(dscore)
    query_rows = jnp.concatenate([queries[0, :, cols(r)] for r in heads], axis=0)
    cotan_rows = jnp.concatenate([cotan[0, :, cols(r)] for r in heads], axis=0)
    key_acc = dot(jnp.concatenate(dscore_heads, axis=0), query_rows, TN)
    value_acc = dot(jnp.concatenate(rounded_heads, axis=0), cotan_rows, TN)
    if sums is not None:
        key_acc, value_acc = key_acc + sums[0], value_acc + sums[1]
    return key_acc, value_acc


def half_body(peers, *refs):
    near = refs[4 : 4 + peers]
    query_grad, sums = refs[4 + peers :]
    sums[0], sums[1] = attend_heads(peers, range(HEADS // 2), *refs[:4], near, query_grad, None)


def attend_body(peers, *refs):
    near = refs[4 : 4 + peers]
    sums, query_grad, own, *parts = refs[4 + peers :]
    key_acc, value_acc = attend_heads(
        peers, range(HEADS // 2, HEADS), *refs[:4], near, query_grad, sums
    )
    own[0:W, :] = key_acc[0:W]
    own[W : 2 * W, :] = value_acc[0:W]
    for k in range(1, peers + 1):
        parts[k - 1][0:W, :] = key_acc[cols(k)].astype(BF16)
        parts[k - 1][W : 2 * W, :] = value_acc[cols(k)].astype(BF16)


def sigmoid(v):
    return 0.5 * jnp.tanh(0.5 * v) + 0.5


def convolve(weight, place, g, count=W):
    total = place[5 : 5 + count, :] * weight[0:1, cols(g)]
    for offset in range(1, TAPS):
        at = 5 + offset
        total = total + place[at : at + count, :] * weight[offset : offset + 1, cols(g)]
    return total


def step_table(pieces, bias, rate):
    slots = len(pieces)
    raw = jnp.concatenate(pieces, axis=0) + jnp.concatenate([bias] * slots, axis=0)
    sizes = jnp.maximum(raw, 0.0) + jnp.log(1.0 + jnp.exp(-jnp.abs(raw)))
    decays = sizes * jnp.concatenate([rate] * slots, axis=0)
    upto = (iota2(0) <= iota2(1)).astype(F32)
    return raw, sizes, dot(decays, upto, precise=True)


def as_columns(table):
    used = HEADS * len(table)
    columns = jnp.transpose(jnp.concatenate(table + [jnp.zeros((W - used, W), F32)], axis=0))

    def column(group, h):
        at = HEADS * group + h
        return columns[:, at : at + 1]

    return column


def with_sum(sums, kind, h, array):
    lane = lax.broadcasted_iota(jnp.int32, sums.shape, 1)
    return jnp.where(lane == HEADS * kind + h, jnp.sum(array, axis=1, keepdims=True), sums)


def join(top, rest):
    return jnp.concatenate([top, rest], axis=0)


def own_body(mixer, step, weight, consts, cotan, *outs):
    ext, acts, slopes, mixed_out, maps, rows_out = outs
    first = iota2(0) < TAPS - 1
    for g in range(GROUPS):
        place = ext.at[g]
        place[0:8, :] = jnp.zeros((8, W), F32)
        place[8 : 8 + W, :] = mixer[0, :, cols(g)].astype(F32)
        pre = convolve(weight, place, g)
        sig = sigmoid(pre)
        acts[g] = jnp.where(first, 0.0, pre * sig)
        slopes[g] = sig + pre * sig * (1.0 - sig)
    _, size, cum = step_table([step[0]], consts[4:8], consts[0:4])
    column = as_columns([cum, size])
    map_in_s, map_out_s = split(acts[HEADS]), split(acts[HEADS + 1])
    meets = dot_split(map_in_s, map_out_s, NT)
    upper = iota2(0) <= iota2(1)
    grad_meets = jnp.zeros((W, W), F32)
    sums = jnp.zeros((W, W), F32)
    out_rows, skip_rows = [], []
    for h in range(HEADS):
        cot_b = cotan[0, :, cols(h)]
        act = acts[h]
        falloff = jnp.where(upper, jnp.exp(cum[h : h + 1] - column(0, h)), 0.0)
        pair = dot_split(split(act * column(1, h)), cot_b, NT) * falloff
        grad_meets = grad_meets + pair
        flow = pair * meets
        mixed = dot_split(split(falloff * meets), cot_b)
        mixed_out[h] = mixed
        out_rows.append(jnp.sum(flow, axis=0, keepdims=True))
        sums = with_sum(sums, 0, h, -flow)
        sums = with_sum(sums, 2, h, mixed * act)
        skip_rows.append(jnp.sum(cot_b.astype(F32) * act, axis=0, keepdims=True))
    grad_meets_b = grad_meets.astype(BF16)
    maps[0] = dot(grad_meets_b, map_out_s[0])
    maps[1] = dot(grad_meets_b, map_in_s[0], TN)
    sum_rows = jnp.transpose(sums)
    rows_out[...] = jnp.concatenate(out_rows + skip_rows + [sum_rows[0 : 4 * HEADS]], axis=0)


def mixer_body(peers, *refs):
    mixer, step, weight, consts, cotan = refs[:5]
    ext, acts, slopes, mixed_in, maps, rows_in = refs[5:11]
    bulk = refs[11 : 11 + peers]
    grads, halo, pay = refs[11 + peers : 14 + peers]
    tails, first_ext, peer_ext, states, adjoints, sums, reads, turned = refs[14 + peers :]
    me = lax.axis_index("ctx")
    slots = peers + 1
    index = [me] + [jnp.bitwise_xor(me, k) for k in range(1, slots)]

    tails[0] = jnp.zeros((16 * GROUPS, W), BF16)
    for g in range(GROUPS):
        tails[me + 1, 16 * g : 16 * g + 16, :] = mixer[0, W - 16 : W, cols(g)]
    for k in range(1, slots):
        earlier = index[k] < me

        @pl.when(earlier)
        def _(k=k):
            for g in range(HEADS + 1):
                tails[index[k] + 1, 16 * g : 16 * g + 16, :] = bulk[k - 1][
                    (g + 1) * W - 16 : (g + 1) * W, :
                ]
            tails[index[k] + 1, 16 * (GROUPS - 1) : 16 * GROUPS, :] = bulk[k - 1][
                STEP_ROW:BULK_ROWS, :
            ]

        @pl.when(jnp.logical_not(earlier))
        def _(k=k):
            tails[index[k] + 1, 16 * (GROUPS - 1) : 16 * GROUPS, :] = bulk[k - 1][
                STEP_ROW - 16 : STEP_ROW, :
            ]

    pieces = [step[0]]
    for k in range(1, slots):
        sent = bulk[k - 1][STEP_ROW:BULK_ROWS, :].astype(F32)
        pieces.append(sent[0:4] + sent[4:8] + sent[8:12])
    rate, bias = consts[0:4], consts[4:8]
    raw, sizes, cumulative = step_table(pieces, bias, rate)

    def rows_of(array, k):
        return array[HEADS * k : HEADS * (k + 1)]

    totals = [
        jnp.broadcast_to(rows_of(cumulative, k)[:, W - 1 : W], (HEADS, W)) for k in range(slots)
    ]
    own_cum = rows_of(cumulative, 0)
    own_size = rows_of(sizes, 0)
    table = [own_cum, own_size, jnp.exp(own_cum), jnp.exp(totals[0] - own_cum)]
    for k in range(1, slots):
        low, high = jnp.minimum(me, index[k]), jnp.maximum(me, index[k])
        between = jnp.zeros((HEADS, W), F32)
        for m in range(1, slots):
            inside = jnp.logical_and(index[m] > low, index[m] < high)
            between = between + jnp.where(inside, totals[m], 0.0)
        earlier = index[k] < me
        cum = rows_of(cumulative, k)
        span = jnp.where(earlier, totals[k] - cum, cum) + between
        table.append(jnp.exp(span) * jnp.where(earlier, rows_of(sizes, k), 1.0))
    column = as_columns(table)

    def peer_act(k, at, g):
        place = peer_ext.at[(k - 1) * GROUPS + g]
        place[0:8, :] = tails[index[k], 16 * g : 16 * g + 16, :].astype(F32)[8:16]
        place[8 : 8 + W, :] = bulk[k - 1][cols(at), :].astype(F32)
        pre = convolve(weight, place, g)
        return pre * sigmoid(pre)

    states[...] = jnp.zeros_like(states)
    adjoints[...] = jnp.zeros_like(adjoints)
    for k in range(1, slots):
        earlier = index[k] < me

        @pl.when(earlier)
        def _(k=k):
            map_in = split(jnp.transpose(peer_act(k, HEADS, HEADS)))
            for h in range(HEADS):
                rows = split(peer_act(k, h, h) * column(3 + k, h))
                states[h] = states[h] + dot_split(map_in, rows)

        @pl.when(jnp.logical_not(earlier))
        def _(k=k):
            map_out = jnp.transpose(peer_act(k, HEADS, HEADS + 1))
            for h in range(HEADS):
                read = split(map_out * table[3 + k][h : h + 1])
                adjoints[h] = adjoints[h] + dot_split(read, bulk[k - 1][cols(h), :])

    early = lax.broadcasted_iota(jnp.int32, (8, W), 0) < TAPS - 1
    first_acts, first_slopes, new_acts = [], [], []
    for g in range(GROUPS):
        place = first_ext.at[g]
        place[0:8, :] = tails[me, 16 * g : 16 * g + 16, :].astype(F32)[8:16]
        place[8:16, :] = ext[g, 8:16, :]
        pre = convolve(weight, place, g, 8)
        sig = sigmoid(pre)
        first_acts.append(pre * sig)
        first_slopes.append(sig + pre * sig * (1.0 - sig))
        new_acts.append(jnp.where(early, pre * sig, 0.0))

    def act_of(g):
        return join(first_acts[g], acts[g, 8:W, :])

    def slope_of(g):
        return join(first_slopes[g], slopes[g, 8:W, :])

    map_in, map_out = act_of(HEADS), act_of(HEADS + 1)
    map_in_s, map_out_s = split(map_in), split(map_out)
    new_in = new_acts[HEADS]
    new_meets = dot_split(split(new_in), map_out_s, NT)
    upper = lax.broadcasted_iota(jnp.int32, (8, W), 0) <= lax.broadcasted_iota(
        jnp.int32, (8, W), 1
    )
    grad_in, grad_out = maps[0], maps[1]
    new_grad_meets = jnp.zeros((8, W), F32)
    sums[...] = jnp.zeros((W, W), F32)
    out_rows, pass_rows, skip_rows = [], [], []

    for h in range(HEADS):
        cot_b = cotan[0, :, cols(h)]
        cot = cot_b.astype(F32)
        act = act_of(h)
        new_act = new_acts[h]
        size = column(1, h)
        tail = column(3, h)
        state = states[h]
        adjoint = adjoints[h]
        adjoint_s = split(adjoint)
        falloff = jnp.where(upper, jnp.exp(own_cum[h : h + 1] - column(0, h)[0:8]), 0.0)
        pair = dot_split(split(new_act * size[0:8]), cot_b, NT) * falloff
        new_grad_meets = new_grad_meets + pair
        flow = pair * new_meets
        new_mixed = dot_split(split(falloff * new_meets), cot_b)
        projected = tail * dot_split(map_in_s, adjoint_s)
        mixed = mixed_in[h]
        mixed = join(mixed[0:8] + new_mixed, mixed[8:W])
        grad_scaled = mixed + projected
        lead_read = column(2, h) * dot_split(cot_b, split(state), NT)
        grad_out = grad_out + lead_read
        reads[:, cols(h)] = (act * size * tail).astype(BF16)
        turned[:, cols(h)] = adjoint_s[0]
        out_rows.append(rows_in[h : h + 1] + jnp.sum(flow, axis=0, keepdims=True))
        carried = lead_read * map_out
        trailing = projected * act
        carried = join(carried[0:8] - flow, carried[8:W])
        sums[:, h : h + 1] = jnp.sum(carried, axis=1, keepdims=True)
        at = HEADS + h
        sums[:, at : at + 1] = jnp.sum(trailing, axis=1, keepdims=True)
        at = 2 * HEADS + h
        sums[0:8, at : at + 1] = jnp.sum(new_mixed * new_act, axis=1, keepdims=True)
        passed = jnp.sum(jnp.sum(state * adjoint, axis=0, keepdims=True), axis=1, keepdims=True)
        pass_rows.append(jnp.broadcast_to(passed, (1, W)))
        skipped = jnp.sum(cot[0:8] * new_act, axis=0, keepdims=True)
        skip_rows.append(rows_in[HEADS + h : HEADS + h + 1] + skipped)
        grads[h, 0:W, :] = (consts[8 + h : 9 + h] * cot + grad_scaled * size) * slope_of(h)
    grad_in = grad_in + dot(reads[...], turned[...], NT)
    new_b = new_grad_meets.astype(BF16)
    grad_out = grad_out + dot(new_b, new_in.astype(BF16), TN)
    grad_in = join(grad_in[0:8] + dot(new_b, map_out_s[0]), grad_in[8:W])
    grads[HEADS, 0:W, :] = grad_in * slope_of(HEADS)
    grads[HEADS + 1, 0:W, :] = grad_out * slope_of(HEADS + 1)
    sum_rows = jnp.transpose(sums[...])

    since = (iota2(0) >= iota2(1)).astype(F32)
    before = (iota2(0) < iota2(1)).astype(F32)
    trail = rows_of(sum_rows, 1)
    grad_decay = (
        dot(
            jnp.concatenate(out_rows, axis=0) + rows_of(sum_rows, 0) + rows_in[8:12],
            since,
            precise=True,
        )
        + dot(trail * own_size, before, precise=True)
        + jnp.exp(totals[0]) * jnp.concatenate(pass_rows, axis=0)
    )
    grad_step = grad_decay * rate + rows_of(sum_rows, 2) + rows_in[16:20] + trail
    grad_raw = grad_step * sigmoid(rows_of(raw, 0))
    pay[24:28, :] = grad_decay * own_size * rate
    pay[28:32, :] = grad_raw
    pay[32:36, :] = jnp.concatenate(skip_rows, axis=0)
    pay[36:40, :] = jnp.zeros((4, W), F32)

    for g in range(GROUPS):
        halo[8 * g : 8 * g + 8, :] = grads[g, 0:8, :]
    for g in range(GROUPS):
        grads[g, W : W + 8, :] = jnp.zeros((8, W), F32)
        grad = grads[g, 0:W, :]
        for offset in range(TAPS):
            pay[4 * g + offset : 4 * g + offset + 1, :] = jnp.sum(
                grad * join(
                    first_ext[g, 5 + offset : 13 + offset, :],
                    ext[g, 13 + offset : 5 + offset + W, :],
                ),
                axis=0,
                keepdims=True,
            )


def rows_body(grads, weight, pay, input_grad, edge, step_grad):
    step_grad[0] = pay[28:32, :]
    for g in range(GROUPS):
        total = grads[g, TAPS - 1 : TAPS - 1 + W, :] * weight[0:1, cols(g)]
        for offset in range(1, TAPS):
            at = TAPS - 1 - offset
            total = total + grads[g, at : at + W, :] * weight[offset : offset + 1, cols(g)]
        input_grad[0, :, cols(g)] = total.astype(BF16)
        edge[:, cols(g)] = total[W - 16 : W]


def merge_body(peers, *refs):
    pay, other, halo = refs[:3]
    parts = refs[3 : 3 + peers]
    total_out, *mixed = refs[3 + peers :]
    total = pay[...] + other[...]
    total_out[...] = total
    sums = total[0:SUM_ROWS]
    high = sums.astype(BF16).astype(F32)
    edges = [halo[8 * g : 8 * g + 3, :] for g in range(GROUPS)]
    rest = jnp.zeros((MIX_ROWS - KV_ROWS - 2 * SUM_ROWS - 3 * GROUPS, W), F32)
    pieces = jnp.concatenate([high, sums - high] + edges + [rest], axis=0).astype(BF16)
    for part, out in zip(parts, mixed):
        out[0:KV_ROWS, :] = part[...]
        out[KV_ROWS:MIX_ROWS, :] = pieces


def finish_body(peers, count, *refs):
    partial, edge, weight, own, pay, half_a, half_b = refs[:7]
    mixed = refs[7 : 7 + peers]
    input_grad, key_grad, value_grad, conv_grad, query_grad, *sums_out = refs[7 + peers :]
    decay_grad, bias_grad, skip_grad = sums_out
    query_grad[0, :, 0 : HEADS // 2 * W] = half_a[0]
    query_grad[0, :, HEADS // 2 * W : HEADS * W] = half_b[0]
    me = lax.axis_index("ctx")
    both = own[...]
    total = pay[0:SUM_ROWS, :]
    halo = jnp.zeros((3 * GROUPS, W), F32)
    for k in range(1, peers + 1):
        other = jnp.bitwise_xor(me, k)
        sent = mixed[k - 1][0:KV_ROWS, :].astype(F32)
        both = both + jnp.where(other > me, sent, 0.0)
        pieces = mixed[k - 1][KV_ROWS:MIX_ROWS, :].astype(F32)
        total = total + pieces[0:SUM_ROWS] + pieces[SUM_ROWS : 2 * SUM_ROWS]
        edges = pieces[2 * SUM_ROWS : 2 * SUM_ROWS + 3 * GROUPS]
        halo = halo + jnp.where(other == me + 1, edges, 0.0)
    key_grad[0] = both[0:W].astype(BF16)
    value_grad[0] = both[W : 2 * W].astype(BF16)
    row = lax.broadcasted_iota(jnp.int32, (16, W), 0)
    for g in range(GROUPS):
        rows = edge[:, cols(g)]
        for offset in range(TAPS - 1):
            for t in range(TAPS - 1 - offset):
                at = 16 - (TAPS - 1 - offset) + t
                piece = halo[3 * g + t : 3 * g + t + 1] * weight[offset : offset + 1, cols(g)]
                rows = rows + jnp.where(row == at, piece, 0.0)
        input_grad[0, 0 : W - 16, cols(g)] = partial[0, 0 : W - 16, cols(g)]
        input_grad[0, W - 16 : W, cols(g)] = rows.astype(BF16)
    total = total * (1.0 / count)
    for g in range(GROUPS):
        conv_grad[:, cols(g)] = total[4 * g : 4 * g + 4]
    sums = jnp.sum(total[24:SUM_ROWS], axis=1, keepdims=True)
    for h in range(HEADS):
        decay_grad[h] = jnp.sum(sums[h : h + 1])
        bias_grad[h] = jnp.sum(sums[4 + h : 5 + h])
        skip_grad[h] = jnp.sum(sums[8 + h : 9 + h])


def shape(dims, dtype):
    return jax.ShapeDtypeStruct(dims, dtype)


def on_device(sizes, *args):
    (
        mixer_input,
        step_input,
        conv_weight,
        decay_log,
        step_bias,
        residual,
        mixer_cotangent,
        queries,
        attn_keys,
        attn_values,
        attn_cotangent,
    ) = args
    ctx, dp = sizes["ctx"], sizes["dp"]
    step_input = jnp.swapaxes(step_input, 1, 2)
    peers = ctx - 1
    bits = ctx.bit_length() - 1
    vmem = pl.BlockSpec(memory_space=pltpu.VMEM)
    smem = pl.BlockSpec(memory_space=pltpu.SMEM)

    hbm = pl.BlockSpec(memory_space=pltpu.HBM)
    params = pltpu.CompilerParams(vmem_limit_bytes=LIMIT)
    near, *bulk, consts = pl.pallas_call(
        lambda *refs: pack_body(bits, *refs),
        out_shape=[shape((KV_ROWS, W), BF16)] + [shape((BULK_ROWS, W), BF16)] * bits
        + [shape((4 * HEADS, W), F32)],
        in_specs=[hbm] * 8,
        out_specs=[vmem] * (2 + bits),
        scratch_shapes=[
            pltpu.VMEM((HEADS, W), F32),
            pltpu.VMEM((16, W), BF16),
            pltpu.VMEM((16, W), BF16),
            pltpu.SMEM((3, HEADS), F32),
            pltpu.SemaphoreType.DMA((7 + bits * (GROUPS + 7),)),
        ],
        compiler_params=params,
        name="pack",
    )(
        *(
            pltpu.with_memory_space_constraint(array, pltpu.HBM)
            for array in (
                mixer_input,
                step_input,
                mixer_cotangent,
                attn_keys,
                attn_values,
                decay_log,
                step_bias,
                residual,
            )
        )
    )

    def swap(array, k, keep=lambda i, j: True, axis="ctx"):
        pairs = [(i, i ^ k) for i in range(sizes[axis]) if keep(i, i ^ k)]
        return lax.ppermute(array, axis, pairs)

    nears = [swap(near, k, lambda i, j: j > i) for k in range(1, ctx)]
    bulks = [swap(bulk[k.bit_length() - 1], k) for k in range(1, ctx)]

    kept = pl.pallas_call(
        own_body,
        out_shape=[
            shape((GROUPS, W + 8, W), F32),
            shape((GROUPS, W, W), F32),
            shape((GROUPS, W, W), F32),
            shape((HEADS, W, W), F32),
            shape((2, W, W), F32),
            shape((6 * HEADS, W), F32),
        ],
        in_specs=[vmem] * 5,
        out_specs=[vmem] * 6,
        compiler_params=params,
        name="own",
    )(
        mixer_input,
        step_input,
        conv_weight,
        consts,
        mixer_cotangent,
    )

    grads, halo, pay = pl.pallas_call(
        lambda *refs: mixer_body(peers, *refs),
        out_shape=[
            shape((GROUPS, W + 8, W), F32),
            shape((8 * GROUPS, W), F32),
            shape((PAY_ROWS, W), F32),
        ],
        in_specs=[vmem] * (11 + peers),
        out_specs=[vmem] * 3,
        scratch_shapes=[
            pltpu.VMEM((ctx + 1, 16 * GROUPS, W), BF16),
            pltpu.VMEM((GROUPS, 24, W), F32),
            pltpu.VMEM((peers * GROUPS, W + 8, W), F32),
            pltpu.VMEM((HEADS, W, W), F32),
            pltpu.VMEM((HEADS, W, W), F32),
            pltpu.VMEM((W, W), F32),
            pltpu.VMEM((W, HEADS * W), BF16),
            pltpu.VMEM((W, HEADS * W), BF16),
        ],
        compiler_params=params,
        name="mixer",
    )(
        mixer_input,
        step_input,
        conv_weight,
        consts,
        mixer_cotangent,
        *kept,
        *bulks,
    )

    input_grad, edge, step_grad = pl.pallas_call(
        rows_body,
        out_shape=[
            shape(mixer_input.shape, BF16),
            shape((16, GROUPS * W), F32),
            shape(step_input.shape, F32),
        ],
        in_specs=[vmem] * 3,
        out_specs=[vmem] * 3,
        compiler_params=params,
        name="rows",
    )(grads, conv_weight, pay)

    half_a, sums = pl.pallas_call(
        lambda *refs: half_body(peers, *refs),
        out_shape=[
            shape((1, W, HEADS // 2 * W), BF16),
            shape((2, ctx * W, W), F32),
        ],
        in_specs=[vmem] * (4 + peers),
        out_specs=[vmem] * 2,
        compiler_params=params,
        name="half",
    )(queries, attn_keys, attn_values, attn_cotangent, *nears)

    half_b, own, *parts = pl.pallas_call(
        lambda *refs: attend_body(peers, *refs),
        out_shape=[shape((1, W, HEADS // 2 * W), BF16), shape((KV_ROWS, W), F32)]
        + [shape((KV_ROWS, W), BF16)] * peers,
        in_specs=[vmem] * (5 + peers),
        out_specs=[vmem] * (2 + peers),
        compiler_params=params,
        name="attend",
    )(queries, attn_keys, attn_values, attn_cotangent, *nears, sums)

    last = dp.bit_length() - 2
    for n in range(last + 1):
        other = swap(pay, 1 << n, axis="dp")
        if n < last:
            pay = pay + other
    pay, *mixed = pl.pallas_call(
        lambda *refs: merge_body(peers, *refs),
        out_shape=[shape((PAY_ROWS, W), F32)] + [shape((MIX_ROWS, W), BF16)] * peers,
        in_specs=[vmem] * (3 + peers),
        out_specs=[vmem] * (1 + peers),
        compiler_params=params,
        name="merge",
    )(pay, other, halo, *parts)
    mixed = [swap(mixed[k - 1], k) for k in range(1, ctx)]
    outs = pl.pallas_call(
        lambda *refs: finish_body(peers, dp, *refs),
        out_shape=[
            shape(mixer_input.shape, BF16),
            shape(attn_keys.shape, BF16),
            shape(attn_values.shape, BF16),
            shape(conv_weight.shape, F32),
            shape(queries.shape, BF16),
        ]
        + [shape((HEADS,), F32)] * 3,
        in_specs=[vmem] * (7 + peers),
        out_specs=[vmem] * 5 + [smem] * 3,
        compiler_params=params,
        name="finish",
    )(input_grad, edge, conv_weight, own, pay, half_a, half_b, *mixed)
    input_grad, key_grad, value_grad, conv_grad, query_grad, *sums_out = outs
    decay_grad, bias_grad, skip_grad = sums_out
    return (
        input_grad,
        jnp.swapaxes(step_grad, 1, 2),
        conv_grad,
        decay_grad,
        bias_grad,
        skip_grad,
        query_grad,
        key_grad,
        value_grad,
    )


def solution(mesh):
    split = P("dp", "ctx", None)
    sizes = dict(mesh.shape)

    def step(*args):
        return on_device(sizes, *args)

    return jax.shard_map(
        step,
        mesh=mesh,
        in_specs=(split, split, P(), P(), P(), P(), split, split, split, split, split),
        out_specs=(split, split, P(), P(), P(), P(), split, split, split),
        check_vma=False,
    )
```
